32 devices in a mesh: grp: 4 (over y, core), gx: 4 (over z), gy: 2 (over x).
Axes of the slice: x: 2, y: 2, z: 4, core: 2. Of those that a mesh axis runs over, the one named last changes fastest.
Arguments:
- previous: float32 [2, 8, 384, 256], P(None, 'grp', 'gx', 'gy'), may hold values from -6 to 6
- current: float32 [2, 8, 384, 256], P(None, 'grp', 'gx', 'gy'), may hold values from -6 to 6
- coeff: float32 [3, 8, 384, 256], P(None, 'grp', 'gx', 'gy'), may hold values from 0.05 to 0.2
- src_index: int32 [1], replicated, may hold values from 0 to 786431
- src_amp: float32 [2, 1], replicated, may hold values from -8 to 8
- rec_index: int32 [2048], replicated, may hold values from 0 to 786431
- rec_amp: float32 [2, 2048], replicated, may hold values from -8 to 8
- offsets: int32 [17], replicated, may hold values from -8 to 8, as said below
Outputs:
- images: float32 [17, 8, 384, 256], P(None, 'grp', ('gx', 'gy'))
- advanced: float32 [2, 8, 384, 256], P(None, 'grp', 'gx', 'gy')
The draws below stay inside these ranges and needn't reach their ends.
Inputs may be any that keep to these rules, and one draw needn't show every extreme that they name: `offsets`: each whole number from -8 to 8 appears exactly once.
All inputs are finite; a program needn't handle non-finite values.
Results may differ from the reference program's by a relative error of at most 0.0003.
Values sent between devices are 32-bit elements; how exact they have to be, the bound alone decides.
No kernel may reach another device: no remote copies, remote signals or barrier semaphores. Data moves between devices by JAX's collectives and lax.ppermute only.
A program may use at most 64 MiB of HBM per device.

```python
import math
import jax
import jax.numpy as jnp
from jax import lax

STEPS = 2
NOFF = 17
MAXOFF = 8
NSRC = 1
NREC = 2048
L = 8
NX = 384
NY = 256


def draw_offsets(key, part):
    return (jax.random.permutation(key, NOFF) - MAXOFF).astype(jnp.int32)


def touch_ends(drawn, rng, least, high):
    shape = drawn.shape
    spot = [jax.random.randint(jax.random.fold_in(rng, axis), (), 0, shape[axis]) for axis in range(len(shape))]
    drawn = drawn.at[tuple(spot)].set(least)
    longest = shape.index(max(shape))
    spot[longest] = (spot[longest] + 1) % shape[longest]
    return drawn.at[tuple(spot)].set(high)


def block_levels(key, dims, shards, smallest, largest):
    def one(position, blocks):
        steps = jax.random.uniform(jax.random.fold_in(jax.random.fold_in(key, 6), position), (blocks,), jnp.float32, smallest / len(shards), largest / len(shards))
        return jnp.repeat(jnp.exp(steps), dims[position] // blocks).reshape((-1,) + (1,) * (len(dims) - position - 1))

    gain = one(*shards[0])
    for cut in shards[1:]:
        gain = gain * one(*cut)
    return gain


def gaussian(own_key, dims, deviation, bound, pieces=(), held_as=jnp.bfloat16):
    gain = block_levels(own_key, dims, pieces, -0.22, 0.18) if pieces else 1.0
    drawn = jax.random.normal(own_key, dims, jnp.float32) * deviation * gain
    return jnp.minimum(jnp.maximum(drawn, -bound), bound).astype(held_as)


def setup_inputs(seed: int = 0) -> dict:
    seeds = jax.random.split(jax.random.key(seed), 9)
    previous = gaussian(seeds[0], (2, L, NX, NY), 1.0, 6.0, ((1, 4), (2, 4), (3, 2)), jnp.float32)
    current = gaussian(seeds[1], (2, L, NX, NY), 1.0, 6.0, ((1, 4), (2, 4), (3, 2)), jnp.float32)
    coeff = jnp.clip(jnp.exp(math.log(0.2) - 1.3862944 * jax.random.uniform(seeds[2], (3, L, NX, NY), jnp.float32) ** block_levels(seeds[2], (3, L, NX, NY), ((1, 4), (2, 4), (3, 2)), -0.2, 0.2)), 0.05, 0.2)
    src_index = jax.random.randint(seeds[3], (NSRC,), 0, L * NX * NY).astype(jnp.int32)
    src_amp = gaussian(seeds[4], (STEPS, NSRC), 2.0, 8.0, (), jnp.float32)
    rec_index = touch_ends(jax.random.randint(seeds[5], (NREC,), 0, L * NX * NY), jax.random.fold_in(seeds[5], 1), 0, (L * NX * NY) - 1).astype(jnp.int32)
    rec_amp = gaussian(seeds[6], (STEPS, NREC), 2.0, 8.0, (), jnp.float32)
    offsets = draw_offsets(jax.random.fold_in(seeds[8], 71), 0)
    return dict(previous=previous, current=current, coeff=coeff, src_index=src_index, src_amp=src_amp, rec_index=rec_index, rec_amp=rec_amp, offsets=offsets)


STENCIL = (-205.0 / 72.0, 8.0 / 5.0, -1.0 / 5.0, 8.0 / 315.0, -1.0 / 560.0)


def laplace(cur, coeff):
    rows_pad = jnp.pad(cur, ((0, 0), (0, 0), (4, 4), (0, 0)))
    cols_pad = jnp.pad(cur, ((0, 0), (0, 0), (0, 0), (4, 4)))
    lays_pad = jnp.pad(cur, ((0, 0), (1, 1), (0, 0), (0, 0)))
    dxx = STENCIL[0] * cur
    dyy = STENCIL[0] * cur
    for j in range(1, 5):
        dxx = dxx + STENCIL[j] * (rows_pad[:, :, 4 + j:4 + j + NX] + rows_pad[:, :, 4 - j:4 - j + NX])
        dyy = dyy + STENCIL[j] * (cols_pad[:, :, :, 4 + j:4 + j + NY] + cols_pad[:, :, :, 4 - j:4 - j + NY])
    dzz = lays_pad[:, 2:] + lays_pad[:, :-2] - 2.0 * cur
    return coeff[0] * dxx + coeff[1] * dyy + coeff[2] * dzz


def inject(field, index, amp):
    return field.reshape(-1).at[index].add(amp).reshape(field.shape)


def reference(previous, current, coeff, src_index, src_amp, rec_index, rec_amp, offsets):
    prev, cur = previous, current
    sources = []
    receivers = []
    for step in range(STEPS):
        nxt = 2.0 * cur - prev + laplace(cur, coeff)
        src_field = inject(nxt[0], src_index, src_amp[step])
        rec_field = inject(nxt[1], rec_index, rec_amp[step])
        nxt = jnp.stack([src_field, rec_field])
        sources.append(src_field)
        receivers.append(rec_field)
        prev, cur = cur, nxt
    source = jnp.stack(sources)
    receiver = jnp.stack(receivers)
    padded = jnp.pad(receiver, ((0, 0), (0, 0), (MAXOFF, MAXOFF), (0, 0)))

    def one_image(offset):
        start = (offset + MAXOFF).astype(jnp.int32)
        moved = lax.dynamic_slice_in_dim(padded, start, NX, axis=2)
        return jnp.sum(source * moved, axis=0)

    images = lax.map(one_image, offsets)
    return images, cur
```

```python
import functools

import jax
import jax.numpy as jnp
from jax import lax
from jax.experimental import pallas as pl
from jax.experimental.pallas import tpu as pltpu
from jax.sharding import PartitionSpec as P

STEPS = 2
NOFF = 17
MAXOFF = 8
REACH = 4


STENCIL = (-205.0 / 72.0, 8.0 / 5.0, -1.0 / 5.0, 8.0 / 315.0, -1.0 / 560.0)


def padded_2(block, sides, width):
    for axis, dim in sides:
        count = lax.axis_size(axis)
        forward = [(i, i + 1) for i in range(count - 1)]
        backward = [(target, source) for source, target in forward]
        low = lax.ppermute(
            lax.slice_in_dim(block, block.shape[dim] - width, None, axis=dim), axis, forward
        )
        high = lax.ppermute(lax.slice_in_dim(block, 0, width, axis=dim), axis, backward)
        block = jnp.concatenate([low, block, high], axis=dim)
    return block


def laplace(cur, coeff):
    wide = padded_2(cur, (("gx", 2), ("gy", 3)), 4)
    deep = padded_2(cur, (("grp", 1),), 1)
    rows = cur.shape[2]
    cols = cur.shape[3]
    dxx = STENCIL[0] * cur
    dyy = STENCIL[0] * cur
    for j in range(1, 5):
        dxx = dxx + STENCIL[j] * (
            wide[:, :, 4 + j : 4 + j + rows, 4 : 4 + cols]
            + wide[:, :, 4 - j : 4 - j + rows, 4 : 4 + cols]
        )
        dyy = dyy + STENCIL[j] * (
            wide[:, :, 4 : 4 + rows, 4 + j : 4 + j + cols]
            + wide[:, :, 4 : 4 + rows, 4 - j : 4 - j + cols]
        )
    dzz = deep[:, 2:] + deep[:, :-2] - 2.0 * cur
    return coeff[0] * dxx + coeff[1] * dyy + coeff[2] * dzz


def inject(field, index, amp):
    layers, rows, cols = field.shape
    total_rows = rows * lax.axis_size("gx")
    total_cols = cols * lax.axis_size("gy")
    layer_at = index // (total_rows * total_cols) - lax.axis_index("grp") * layers
    row_at = index // total_cols % total_rows - lax.axis_index("gx") * rows
    col_at = index % total_cols - lax.axis_index("gy") * cols
    inside = (
        (layer_at >= 0)
        & (layer_at < layers)
        & (row_at >= 0)
        & (row_at < rows)
        & (col_at >= 0)
        & (col_at < cols)
    )
    layer_at = jnp.clip(layer_at, 0, layers - 1)
    row_at = jnp.clip(row_at, 0, rows - 1)
    col_at = jnp.clip(col_at, 0, cols - 1)
    return field.at[layer_at, row_at, col_at].add(jnp.where(inside, amp, 0.0))


def correlate(source, padded, offsets, rows):
    pieces = []
    for k in range(NOFF):
        start = offsets[k] + MAXOFF
        moved = lax.dynamic_slice_in_dim(padded, start, rows, axis=2)
        pieces.append(jnp.sum(source * moved, axis=0))
    return jnp.stack(pieces)


def body_tiles(previous, current, coeff, src_index, src_amp, rec_index, rec_amp, offsets):
    prev, cur = (previous, current)
    snapshots = []
    for step in range(STEPS):
        nxt = 2.0 * cur - prev + laplace(cur, coeff)
        src_field = inject(nxt[0], src_index, src_amp[step])
        rec_field = inject(nxt[1], rec_index, rec_amp[step])
        nxt = jnp.stack([src_field, rec_field])
        snapshots.append(nxt)
        prev, cur = (cur, nxt)
    snaps = jnp.stack(snapshots)
    moved = lax.all_to_all(snaps, "gy", split_axis=3, concat_axis=4, tiled=True)
    source = moved[:, 0]
    padded = padded_2(moved[:, 1], ((("gx", "gy"), 2),), MAXOFF)
    images = correlate(source, padded, offsets, source.shape[2])
    return (images, cur)


VMEM = pl.BlockSpec(memory_space=pltpu.VMEM)
SMEM = pl.BlockSpec(memory_space=pltpu.SMEM)
HBM = pl.BlockSpec(memory_space=pl.ANY)


class Plan:
    def __init__(self, shape, mesh_shape):
        self.fields, self.lays, self.rows, self.cols = shape
        self.n_grp, self.n_gx, self.n_gy = (mesh_shape[k] for k in ("grp", "gx", "gy"))
        self.nx = self.rows * self.n_gx
        self.ny = self.cols * self.n_gy
        self.half = self.rows // self.n_gy
        self.d2 = MAXOFF
        self.d1 = MAXOFF + REACH
        self.d0 = MAXOFF + 2 * REACH
        self.inside = self.half + self.d0
        self.e0 = self.half + 2 * self.d0
        self.e1 = self.half + 2 * self.d1
        self.e2 = self.half + 2 * self.d2

    def fits(self):
        return (
            self.n_gy == 2
            and self.n_grp % 2 == 0
            and self.n_gx % 2 == 0
            and self.rows % 16 == 0
            and self.cols % 128 == 0
            and self.inside <= self.rows
            and STEPS == 2
        )

    def base_row(self):
        return lax.axis_index("gx") * self.rows + lax.axis_index("gy") * self.half


def cost(flops, moved):
    return pl.CostEstimate(flops=flops, bytes_accessed=moved, transcendentals=0)


def f32(*shape):
    return jax.ShapeDtypeStruct(shape, jnp.float32)


def pack_kernel(p, count, *refs):
    sources = refs[:count]
    outs = refs[count : count + 4]
    sems = refs[count + 4]
    b = lax.axis_index("gy")
    starts = (
        (b * (p.rows - p.inside), p.inside),
        ((1 - b) * (p.rows - p.inside), p.inside),
        ((1 - b) * (p.rows - p.d0), p.d0),
        (b * (p.rows - p.d0), p.d0),
    )
    copies = []
    plane = 0
    for i, source in enumerate(sources):
        planes = source.shape[0]
        for j, (start, size) in enumerate(starts):
            copies.append(
                pltpu.make_async_copy(
                    source.at[:, pl.ds(pl.multiple_of(start, 8), size), :],
                    outs[j].at[pl.ds(plane, planes)],
                    sems.at[i, j],
                )
            )
        plane += planes
    for copy in copies:
        copy.start()
    for copy in copies:
        copy.wait()


def pack(p, *sources):
    planes = sum(s.shape[0] for s in sources)
    return pl.pallas_call(
        functools.partial(pack_kernel, p, len(sources)),
        out_shape=(
            f32(planes, p.inside, p.cols),
            f32(planes, p.inside, p.cols),
            f32(planes, p.d0, p.cols),
            f32(planes, p.d0, p.cols),
        ),
        in_specs=[HBM] * len(sources),
        out_specs=(VMEM,) * 4,
        scratch_shapes=[pltpu.SemaphoreType.DMA((len(sources), 4))],
        cost_estimate=cost(0, 4 * planes * p.rows * p.cols * 3),
    )(*sources)


def lay_out(p, target, own, other, halo_own, halo_other):
    a = lax.axis_index("gx")
    b = lax.axis_index("gy")
    mine = pl.ds(pl.multiple_of(b * p.cols, p.cols), p.cols)
    theirs = pl.ds(pl.multiple_of((1 - b) * p.cols, p.cols), p.cols)
    inner = pl.ds(pl.multiple_of((1 - b) * p.d0, 8), p.inside)
    outer = pl.ds(pl.multiple_of(b * p.inside, 8), p.d0)
    there = jnp.where(b == 0, a > 0, a < p.n_gx - 1)
    target[:, inner, mine] = own[...]
    target[:, inner, theirs] = other[...]
    target[:, outer, mine] = jnp.where(there, halo_own[...], 0.0)
    target[:, outer, theirs] = jnp.where(there, halo_other[...], 0.0)


def send_layers(p, whole, send_a, send_b, shift, count):
    odd = lax.rem(lax.axis_index("grp"), 2)
    lay_a = (1 - odd) * (p.lays - 1)
    lay_b = odd * (p.lays - 1)
    for f in range(p.fields):
        send_a[f] = whole[f * p.lays + lay_a, shift : shift + count, :]
        send_b[f] = whole[f * p.lays + lay_b, shift : shift + count, :]


def join_kernel(p, own, other, halo_own, halo_other, whole, send_a, send_b):
    lay_out(p, whole, own, other, halo_own, halo_other)
    send_layers(p, whole, send_a, send_b, p.d0 - p.d1, p.e1)


def join(p, own, other, halo_own, halo_other):
    planes = own.shape[0]
    return pl.pallas_call(
        functools.partial(join_kernel, p),
        out_shape=(
            f32(planes, p.e0, p.ny),
            f32(p.fields, p.e1, p.ny),
            f32(p.fields, p.e1, p.ny),
        ),
        in_specs=[VMEM] * 4,
        out_specs=(VMEM,) * 3,
        cost_estimate=cost(0, 8 * planes * p.e0 * p.ny),
    )(own, other, halo_own, halo_other)


def spread_kernel(p, index, amp, out, row_hot, col_hot, total):
    lays, stride = p.lays, p.e0
    g = lax.axis_index("grp")
    first = p.base_row() - p.d1
    wide = index.shape[0]
    grid_row = first + lax.broadcasted_iota(jnp.int32, (stride, 128), 0)
    known = (grid_row >= 0) & (grid_row < p.nx)
    wanted = [
        jnp.where(known, (g * lays + lay) * p.nx + grid_row, -1) for lay in range(lays)
    ]
    column = lax.broadcasted_iota(jnp.int32, (p.ny, 128), 0)
    for k in range(wide):
        at = pl.ds(k * 128, 128)
        flat = index[k : k + 1, :]
        row = jnp.floor((flat.astype(jnp.float32) + 0.5) * (1.0 / p.ny)).astype(jnp.int32)
        col = flat - row * p.ny
        col_hot[:, at] = jnp.where(column == col, 1.0, 0.0).astype(jnp.bfloat16)
        for step in range(STEPS):
            rest = amp[step, k : k + 1, :]
            parts = []
            for _ in range(3):
                part = rest.astype(jnp.bfloat16).astype(jnp.float32)
                parts.append(part)
                rest = rest - part
            for lay in range(lays):
                hit = wanted[lay] == row
                for i, part in enumerate(parts):
                    start = ((step * 3 + i) * lays + lay) * stride
                    row_hot[start : start + stride, at] = jnp.where(
                        hit, part, 0.0
                    ).astype(jnp.bfloat16)
    total[...] = lax.dot_general(
        row_hot[...],
        col_hot[...],
        (((1,), (1,)), ((), ())),
        preferred_element_type=jnp.float32,
    )
    for step in range(STEPS):
        for lay in range(lays):
            rows = [((step * 3 + i) * lays + lay) * stride for i in range(3)]
            out[step, lay] = (
                total[rows[0] : rows[0] + p.e1]
                + total[rows[1] : rows[1] + p.e1]
                + total[rows[2] : rows[2] + p.e1]
            )


def spread(p, index, amp):
    count = index.shape[0]
    wide = -(-count // 128)
    extra = wide * 128 - count
    if extra:
        index = jnp.pad(index, (0, extra))
        amp = jnp.pad(amp, ((0, 0), (0, extra)))
    tall = STEPS * 3 * p.lays * p.e0
    return pl.pallas_call(
        functools.partial(spread_kernel, p),
        out_shape=f32(STEPS, p.lays, p.e1, p.ny),
        in_specs=[VMEM] * 2,
        out_specs=VMEM,
        scratch_shapes=[
            pltpu.VMEM((tall, wide * 128), jnp.bfloat16),
            pltpu.VMEM((p.ny, wide * 128), jnp.bfloat16),
            pltpu.VMEM((tall, p.ny), jnp.float32),
        ],
        cost_estimate=cost(2 * tall * wide * 128 * p.ny, 4 * wide * 128 * 3),
    )(index.reshape(wide, 128), amp.reshape(STEPS, wide, 128))


def advance(p, now, before, before_at, coeff, coeff_at, recv_a, recv_b, added, added_at, out, margin):
    g = lax.axis_index("grp")
    even = lax.rem(g, 2) == 0
    beyond = jnp.where(even, g > 0, g < p.n_grp - 1)
    first = p.base_row() - margin
    count = p.half + 2 * margin
    column = lax.broadcasted_iota(jnp.int32, (8, p.ny), 1)
    line = lax.broadcasted_iota(jnp.int32, (8, p.ny), 0)
    for r in range(0, count, 8):
        rows = slice(r, r + 8)
        weights = [
            [coeff[i * p.lays + lay, coeff_at + r : coeff_at + r + 8, :] for i in range(3)]
            for lay in range(p.lays)
        ]
        edge = r < margin or r + 8 > p.half + margin
        if edge:
            grid_row = first + r + line
            known = (grid_row >= 0) & (grid_row < p.nx)
        for f in range(p.fields):
            far = jnp.where(beyond, recv_b[f, rows, :], 0.0)
            near = recv_a[f, rows, :]
            below = jnp.where(even, far, near)
            above = jnp.where(even, near, far)
            mids = [
                now[f * p.lays + lay, REACH + r : REACH + r + 8, :] for lay in range(p.lays)
            ]
            column_of = [below] + mids + [above]
            for lay in range(p.lays):
                plane = f * p.lays + lay
                x = mids[lay]
                dxx = STENCIL[0] * x
                dyy = STENCIL[0] * x
                for j in range(1, REACH + 1):
                    dxx = dxx + STENCIL[j] * (
                        now[plane, REACH + r + j : REACH + r + j + 8, :]
                        + now[plane, REACH + r - j : REACH + r - j + 8, :]
                    )
                    right = jnp.where(column < p.ny - j, pltpu.roll(x, p.ny - j, 1), 0.0)
                    left = jnp.where(column >= j, pltpu.roll(x, j, 1), 0.0)
                    dyy = dyy + STENCIL[j] * (right + left)
                dzz = column_of[lay] + column_of[lay + 2] - 2.0 * x
                w = weights[lay]
                new = (
                    2.0 * x
                    - before[plane, before_at + r : before_at + r + 8, :]
                    + (w[0] * dxx + w[1] * dyy + w[2] * dzz)
                )
                if f == 1:
                    new = new + added[lay, added_at + r : added_at + r + 8, :]
                if edge:
                    new = jnp.where(known, new, 0.0)
                out[plane, rows, :] = new


def add_source(p, step, index, amp, out, margin):
    g = lax.axis_index("grp")
    first = p.base_row() - margin
    count = p.half + 2 * margin
    for s in range(index.shape[0]):
        flat = index[s]
        line = lax.div(flat, p.ny)
        lay = lax.div(line, p.nx) - g * p.lays
        row = lax.rem(line, p.nx) - first
        col = lax.rem(flat, p.ny)

        @pl.when((lay >= 0) & (lay < p.lays) & (row >= 0) & (row < count))
        def _():
            spot = lax.broadcasted_iota(jnp.int32, (1, p.ny), 1) == col
            out[lay, pl.ds(row, 1), :] += jnp.where(spot, amp[step, s], 0.0)


def first_kernel(
    p, now, recv_a, recv_b, own, other, halo_own, halo_other, added, index, amp,
    out, coeff_out, send_a, send_b, rest,
):
    lay_out(p, rest, own, other, halo_own, halo_other)
    planes = p.fields * p.lays
    gap = p.d0 - p.d1
    coeff_out[...] = rest[planes:, p.d0 - p.d2 : p.d0 - p.d2 + p.e2, :]
    advance(
        p, now, rest, gap, rest.at[planes:], gap, recv_a, recv_b, added.at[0], 0, out, p.d1
    )
    add_source(p, 0, index, amp, out, p.d1)
    send_layers(p, out, send_a, send_b, p.d1 - p.d2, p.e2)


def first_step(p, now, recv_a, recv_b, rest, added, index, amp):
    planes = p.fields * p.lays
    return pl.pallas_call(
        functools.partial(first_kernel, p),
        out_shape=(
            f32(planes, p.e1, p.ny),
            f32(3 * p.lays, p.e2, p.ny),
            f32(p.fields, p.e2, p.ny),
            f32(p.fields, p.e2, p.ny),
        ),
        in_specs=[VMEM] * 8 + [SMEM] * 2,
        out_specs=(VMEM,) * 4,
        scratch_shapes=[pltpu.VMEM((planes + 3 * p.lays, p.e0, p.ny), jnp.float32)],
        cost_estimate=cost(60 * planes * p.e1 * p.ny, 8 * planes * p.e1 * p.ny),
    )(now, recv_a, recv_b, *rest, added, index, amp)


def second_kernel(p, now, before, coeff, recv_a, recv_b, added, index, amp, out, keep, give):
    gap = p.d1 - p.d2
    advance(
        p, now, before, p.d0 - p.d2, coeff, 0, recv_a, recv_b, added.at[1], gap, out, p.d2
    )
    add_source(p, 1, index, amp, out, p.d2)
    b = lax.axis_index("gy")
    mine = pl.ds(pl.multiple_of(b * p.cols, p.cols), p.cols)
    theirs = pl.ds(pl.multiple_of((1 - b) * p.cols, p.cols), p.cols)
    keep[...] = out[:, p.d2 : p.d2 + p.half, mine]
    give[...] = out[:, p.d2 : p.d2 + p.half, theirs]


def second_step(p, now, before, coeff, recv_a, recv_b, added, index, amp):
    planes = p.fields * p.lays
    return pl.pallas_call(
        functools.partial(second_kernel, p),
        out_shape=(
            f32(planes, p.e2, p.ny),
            f32(planes, p.half, p.cols),
            f32(planes, p.half, p.cols),
        ),
        in_specs=[VMEM] * 6 + [SMEM] * 2,
        out_specs=(VMEM,) * 3,
        cost_estimate=cost(60 * planes * p.e2 * p.ny, 8 * planes * p.e2 * p.ny),
    )(now, before, coeff, recv_a, recv_b, added, index, amp)


def image_kernel(p, one, two, offsets, out, held, place, sems):
    for k in range(NOFF):
        place[offsets[k] + MAXOFF] = k
    copies = []
    for d in range(NOFF):
        shift = d - MAXOFF
        for lay in range(p.lays):
            for r in range(0, p.half, 8):
                s1 = one[lay, p.d1 + r : p.d1 + r + 8, :]
                r1 = one[p.lays + lay, p.d1 + r + shift : p.d1 + r + shift + 8, :]
                s2 = two[lay, p.d2 + r : p.d2 + r + 8, :]
                r2 = two[p.lays + lay, p.d2 + r + shift : p.d2 + r + shift + 8, :]
                held[d, lay, r : r + 8, :] = s1 * r1 + s2 * r2
        copy = pltpu.make_async_copy(held.at[d], out.at[place[d]], sems.at[d])
        copy.start()
        copies.append(copy)
    for copy in copies:
        copy.wait()


def correlate_rows(p, one, two, offsets):
    size = NOFF * p.lays * p.half * p.ny
    return pl.pallas_call(
        functools.partial(image_kernel, p),
        out_shape=f32(NOFF, p.lays, p.half, p.ny),
        in_specs=[VMEM] * 2 + [SMEM],
        out_specs=HBM,
        scratch_shapes=[
            pltpu.VMEM((NOFF, p.lays, p.half, p.ny), jnp.float32),
            pltpu.SMEM((NOFF,), jnp.int32),
            pltpu.SemaphoreType.DMA((NOFF,)),
        ],
        cost_estimate=cost(3 * size, 4 * size),
    )(one, two, offsets)


def settle_kernel(p, keep, got, out, sems):
    b = lax.axis_index("gy")
    copies = [
        pltpu.make_async_copy(
            source,
            out.at[:, pl.ds(pl.multiple_of(at * p.half, 8), p.half), :],
            sems.at[i],
        )
        for i, (source, at) in enumerate(((keep, b), (got, 1 - b)))
    ]
    for copy in copies:
        copy.start()
    for copy in copies:
        copy.wait()


def settle(p, keep, got):
    planes = p.fields * p.lays
    return pl.pallas_call(
        functools.partial(settle_kernel, p),
        out_shape=f32(planes, p.rows, p.cols),
        in_specs=[VMEM] * 2,
        out_specs=HBM,
        scratch_shapes=[pltpu.SemaphoreType.DMA((2,))],
        cost_estimate=cost(0, 8 * planes * p.rows * p.cols),
    )(keep, got)


def pairs_grp(p):
    return [(g, g ^ 1) for g in range(p.n_grp)]


def pairs_between(p):
    pairs = []
    for g in range(p.n_grp):
        to = g + 1 if g % 2 else g - 1
        for a in range(p.n_gx):
            goal = (to, a) if 0 <= to < p.n_grp else (g, a ^ 1)
            pairs.append((g * p.n_gx + a, goal[0] * p.n_gx + goal[1]))
    return pairs


def halo_straight(p):
    pairs = []
    for a in range(p.n_gx):
        for b in range(2):
            to = (a + 1 if b == 0 else a - 1) % p.n_gx
            pairs.append((a * 2 + b, to * 2 + b))
    return pairs


def halo_across(p):
    pairs = []
    for a in range(p.n_gx):
        for b in range(2):
            to = (a - 1 if b == 0 else a + 1) % p.n_gx
            pairs.append((a * 2 + b, to * 2 + 1 - b))
    return pairs


def body_rows(p, previous, current, coeff, src_index, src_amp, rec_index, rec_amp, offsets):
    planes = p.fields * p.lays
    tile = (p.rows, p.cols)

    def redistribute(*sources):
        own, give, edge, corner = pack(p, *sources)
        other = lax.ppermute(give, "gy", [(0, 1), (1, 0)])
        halo_own = lax.ppermute(edge, ("gx", "gy"), halo_straight(p))
        halo_other = lax.ppermute(corner, ("gx", "gy"), halo_across(p))
        return own, other, halo_own, halo_other

    def swap_layers(send_a, send_b):
        recv_a = lax.ppermute(send_a, "grp", pairs_grp(p))
        recv_b = lax.ppermute(send_b, ("grp", "gx"), pairs_between(p))
        return recv_a, recv_b

    now = redistribute(current.reshape(planes, *tile))
    rest = redistribute(previous.reshape(planes, *tile), coeff.reshape(3 * p.lays, *tile))
    added = spread(p, rec_index, rec_amp)
    whole, send_a, send_b = join(p, *now)
    recv_a, recv_b = swap_layers(send_a, send_b)
    one, weights, send_a, send_b = first_step(
        p, whole, recv_a, recv_b, rest, added, src_index, src_amp
    )
    recv_a, recv_b = swap_layers(send_a, send_b)
    two, keep, give = second_step(
        p, one, whole, weights, recv_a, recv_b, added, src_index, src_amp
    )
    got = lax.ppermute(give, "gy", [(0, 1), (1, 0)])
    images = correlate_rows(p, one, two, offsets)
    advanced = settle(p, keep, got)
    return images, advanced.reshape(p.fields, p.lays, *tile)


def solution(mesh):
    def body(previous, *others):
        p = Plan(previous.shape, mesh.shape)
        if p.fits():
            return body_rows(p, previous, *others)
        return body_tiles(previous, *others)

    return jax.shard_map(
        body,
        mesh=mesh,
        in_specs=(
            P(None, "grp", "gx", "gy"),
            P(None, "grp", "gx", "gy"),
            P(None, "grp", "gx", "gy"),
            P(),
            P(),
            P(),
            P(),
            P(),
        ),
        out_specs=(P(None, "grp", ("gx", "gy"), None), P(None, "grp", "gx", "gy")),
        check_vma=False,
    )
```

```python
import functools

import jax
import jax.numpy as jnp
from jax import lax
from jax.experimental import pallas as pl
from jax.experimental.pallas import tpu as pltpu
from jax.sharding import PartitionSpec as P


STEPS = 2
NOFF = 17
MAXOFF = 8
REACH = 4


STENCIL = (-205.0 / 72.0, 8.0 / 5.0, -1.0 / 5.0, 8.0 / 315.0, -1.0 / 560.0)


def padded_2(block, sides, width):
    for axis, dim in sides:
        count = lax.axis_size(axis)
        forward = [(i, i + 1) for i in range(count - 1)]
        backward = [(target, source) for source, target in forward]
        low = lax.ppermute(
            lax.slice_in_dim(block, block.shape[dim] - width, None, axis=dim), axis, forward
        )
        high = lax.ppermute(lax.slice_in_dim(block, 0, width, axis=dim), axis, backward)
        block = jnp.concatenate([low, block, high], axis=dim)
    return block


def laplace(cur, coeff):
    wide = padded_2(cur, (("gx", 2), ("gy", 3)), 4)
    deep = padded_2(cur, (("grp", 1),), 1)
    rows = cur.shape[2]
    cols = cur.shape[3]
    dxx = STENCIL[0] * cur
    dyy = STENCIL[0] * cur
    for j in range(1, 5):
        dxx = dxx + STENCIL[j] * (
            wide[:, :, 4 + j : 4 + j + rows, 4 : 4 + cols]
            + wide[:, :, 4 - j : 4 - j + rows, 4 : 4 + cols]
        )
        dyy = dyy + STENCIL[j] * (
            wide[:, :, 4 : 4 + rows, 4 + j : 4 + j + cols]
            + wide[:, :, 4 : 4 + rows, 4 - j : 4 - j + cols]
        )
    dzz = deep[:, 2:] + deep[:, :-2] - 2.0 * cur
    return coeff[0] * dxx + coeff[1] * dyy + coeff[2] * dzz


def inject(field, index, amp):
    layers, rows, cols = field.shape
    total_rows = rows * lax.axis_size("gx")
    total_cols = cols * lax.axis_size("gy")
    layer_at = index // (total_rows * total_cols) - lax.axis_index("grp") * layers
    row_at = index // total_cols % total_rows - lax.axis_index("gx") * rows
    col_at = index % total_cols - lax.axis_index("gy") * cols
    inside = (
        (layer_at >= 0)
        & (layer_at < layers)
        & (row_at >= 0)
        & (row_at < rows)
        & (col_at >= 0)
        & (col_at < cols)
    )
    layer_at = jnp.clip(layer_at, 0, layers - 1)
    row_at = jnp.clip(row_at, 0, rows - 1)
    col_at = jnp.clip(col_at, 0, cols - 1)
    return field.at[layer_at, row_at, col_at].add(jnp.where(inside, amp, 0.0))


def correlate(source, padded, offsets, rows):
    pieces = []
    for k in range(NOFF):
        start = offsets[k] + MAXOFF
        moved = lax.dynamic_slice_in_dim(padded, start, rows, axis=2)
        pieces.append(jnp.sum(source * moved, axis=0))
    return jnp.stack(pieces)


def body_tiles(previous, current, coeff, src_index, src_amp, rec_index, rec_amp, offsets):
    prev, cur = (previous, current)
    snapshots = []
    for step in range(STEPS):
        nxt = 2.0 * cur - prev + laplace(cur, coeff)
        src_field = inject(nxt[0], src_index, src_amp[step])
        rec_field = inject(nxt[1], rec_index, rec_amp[step])
        nxt = jnp.stack([src_field, rec_field])
        snapshots.append(nxt)
        prev, cur = (cur, nxt)
    snaps = jnp.stack(snapshots)
    moved = lax.all_to_all(snaps, "gy", split_axis=3, concat_axis=4, tiled=True)
    source = moved[:, 0]
    padded = padded_2(moved[:, 1], ((("gx", "gy"), 2),), MAXOFF)
    images = correlate(source, padded, offsets, source.shape[2])
    return (images, cur)


VMEM = pl.BlockSpec(memory_space=pltpu.VMEM)
SMEM = pl.BlockSpec(memory_space=pltpu.SMEM)
HBM = pl.BlockSpec(memory_space=pltpu.HBM)
PARAMS = pltpu.CompilerParams(vmem_limit_bytes=16 << 20)


class Plan:
    def __init__(self, shape, mesh_shape):
        self.fields, self.lays, self.rows, self.cols = shape
        self.n_grp, self.n_gx, self.n_gy = (mesh_shape[k] for k in ("grp", "gx", "gy"))
        self.nx = self.rows * self.n_gx
        self.ny = self.cols * self.n_gy
        self.half = self.rows // self.n_gy
        self.d2 = MAXOFF
        self.d1 = MAXOFF + REACH
        self.d0 = MAXOFF + 2 * REACH
        self.inside = self.half + self.d0
        self.e0 = self.half + 2 * self.d0
        self.e1 = self.half + 2 * self.d1
        self.e2 = self.half + 2 * self.d2

    def fits(self):
        return (
            self.n_gy == 2
            and self.n_grp % 2 == 0
            and self.n_gx % 2 == 0
            and self.rows % 16 == 0
            and self.cols % 128 == 0
            and self.inside <= self.rows
            and STEPS == 2
        )

    def base_row(self):
        return lax.axis_index("gx") * self.rows + lax.axis_index("gy") * self.half


def cost(flops, moved):
    return pl.CostEstimate(flops=flops, bytes_accessed=moved, transcendentals=0)


def f32(*shape):
    return jax.ShapeDtypeStruct(shape, jnp.float32)


def pack_kernel(p, count, *refs):
    sources = refs[:count]
    outs = refs[count : count + 4]
    sems = refs[count + 4]
    b = lax.axis_index("gy")
    starts = (
        (b * (p.rows - p.inside), p.inside),
        ((1 - b) * (p.rows - p.inside), p.inside),
        ((1 - b) * (p.rows - p.d0), p.d0),
        (b * (p.rows - p.d0), p.d0),
    )
    copies = []
    plane = 0
    for i, source in enumerate(sources):
        planes = source.shape[0]
        for j, (start, size) in enumerate(starts):
            copies.append(
                pltpu.make_async_copy(
                    source.at[:, pl.ds(pl.multiple_of(start, 8), size), :],
                    outs[j].at[pl.ds(plane, planes)],
                    sems.at[i, j],
                )
            )
        plane += planes
    for copy in copies:
        copy.start()
    for copy in copies:
        copy.wait()


def pack(p, *sources):
    planes = sum(s.shape[0] for s in sources)
    return pl.pallas_call(
        functools.partial(pack_kernel, p, len(sources)),
        out_shape=(
            f32(planes, p.inside, p.cols),
            f32(planes, p.inside, p.cols),
            f32(planes, p.d0, p.cols),
            f32(planes, p.d0, p.cols),
        ),
        in_specs=[HBM] * len(sources),
        out_specs=(VMEM,) * 4,
        scratch_shapes=[pltpu.SemaphoreType.DMA((len(sources), 4))],
        compiler_params=PARAMS,
        cost_estimate=cost(0, 4 * planes * p.rows * p.cols * 3),
    )(*sources)


def lay_out(p, target, own, other, halo_own, halo_other):
    a = lax.axis_index("gx")
    b = lax.axis_index("gy")
    mine = pl.ds(pl.multiple_of(b * p.cols, p.cols), p.cols)
    theirs = pl.ds(pl.multiple_of((1 - b) * p.cols, p.cols), p.cols)
    inner = pl.ds(pl.multiple_of((1 - b) * p.d0, 8), p.inside)
    outer = pl.ds(pl.multiple_of(b * p.inside, 8), p.d0)
    there = jnp.where(b == 0, a > 0, a < p.n_gx - 1)
    target[:, inner, mine] = own[...]
    target[:, inner, theirs] = other[...]
    target[:, outer, mine] = jnp.where(there, halo_own[...], 0.0)
    target[:, outer, theirs] = jnp.where(there, halo_other[...], 0.0)


def send_layers(p, whole, send_a, send_b, shift, count):
    odd = lax.rem(lax.axis_index("grp"), 2)
    lay_a = (1 - odd) * (p.lays - 1)
    lay_b = odd * (p.lays - 1)
    for f in range(p.fields):
        send_a[f] = whole[f * p.lays + lay_a, shift : shift + count, :]
        send_b[f] = whole[f * p.lays + lay_b, shift : shift + count, :]


def join_kernel(p, own, other, halo_own, halo_other, whole, send_a, send_b):
    lay_out(p, whole, own, other, halo_own, halo_other)
    send_layers(p, whole, send_a, send_b, p.d0 - p.d1, p.e1)


def join(p, own, other, halo_own, halo_other):
    planes = own.shape[0]
    return pl.pallas_call(
        functools.partial(join_kernel, p),
        out_shape=(
            f32(planes, p.e0, p.ny),
            f32(p.fields, p.e1, p.ny),
            f32(p.fields, p.e1, p.ny),
        ),
        in_specs=[VMEM] * 4,
        out_specs=(VMEM,) * 3,
        compiler_params=PARAMS,
        cost_estimate=cost(0, 8 * planes * p.e0 * p.ny),
    )(own, other, halo_own, halo_other)


def spread_kernel(p, step, index, amp, src_index, src_amp, out, row_hot, col_hot, total):
    lays, stride = p.lays, p.e0
    g = lax.axis_index("grp")
    first = p.base_row() - p.d1
    wide = index.shape[0]
    grid_row = first + lax.broadcasted_iota(jnp.int32, (stride, 128), 0)
    known = (grid_row >= 0) & (grid_row < p.nx)
    wanted = [
        jnp.where(known, (g * lays + lay) * p.nx + grid_row, -1) for lay in range(lays)
    ]
    column = lax.broadcasted_iota(jnp.int32, (p.ny, 128), 0)
    for k in range(wide):
        at = slice(k * 128, (k + 1) * 128)
        flat = index[k : k + 1, :]
        row = jnp.floor((flat.astype(jnp.float32) + 0.5) * (1.0 / p.ny)).astype(jnp.int32)
        col = flat - row * p.ny
        col_hot[:, at] = jnp.where(column == col, 1.0, 0.0).astype(jnp.bfloat16)
        rest = amp[step : step + 1, at]
        parts = []
        for _ in range(3):
            part = rest.astype(jnp.bfloat16).astype(jnp.float32)
            parts.append(part)
            rest = rest - part
        for lay in range(lays):
            hit = wanted[lay] == row
            for i, part in enumerate(parts):
                start = (i * lays + lay) * stride
                row_hot[start : start + stride, at] = jnp.where(hit, part, 0.0).astype(
                    jnp.bfloat16
                )
    total[...] = lax.dot_general(
        row_hot[...],
        col_hot[...],
        (((1,), (1,)), ((), ())),
        preferred_element_type=jnp.float32,
    )
    for lay in range(lays):
        rows = [(i * lays + lay) * stride for i in range(3)]
        out[1, lay] = (
            total[rows[0] : rows[0] + p.e1]
            + total[rows[1] : rows[1] + p.e1]
            + total[rows[2] : rows[2] + p.e1]
        )
    out[0] = jnp.zeros((lays, p.e1, p.ny), jnp.float32)
    for s in range(src_index.shape[0]):
        flat = src_index[s]
        line = lax.div(flat, p.ny)
        lay = lax.div(line, p.nx) - g * lays
        row = lax.rem(line, p.nx) - first
        col = lax.rem(flat, p.ny)

        @pl.when((lay >= 0) & (lay < lays) & (row >= 0) & (row < p.e1))
        def _():
            spot = lax.broadcasted_iota(jnp.int32, (1, p.ny), 1) == col
            amount = src_amp[step * src_index.shape[0] + s]
            out[0, lay, pl.ds(row, 1), :] += jnp.where(spot, amount, 0.0)


def spread(p, step, index, amp, src_index, src_amp):
    wide = index.shape[0]
    tall = 3 * p.lays * p.e0
    return pl.pallas_call(
        functools.partial(spread_kernel, p, step),
        out_shape=f32(p.fields, p.lays, p.e1, p.ny),
        in_specs=[VMEM] * 2 + [SMEM] * 2,
        out_specs=VMEM,
        scratch_shapes=[
            pltpu.VMEM((tall, wide * 128), jnp.bfloat16),
            pltpu.VMEM((p.ny, wide * 128), jnp.bfloat16),
            pltpu.VMEM((tall, p.ny), jnp.float32),
        ],
        compiler_params=PARAMS,
        cost_estimate=cost(2 * tall * wide * 128 * p.ny, 4 * wide * 128 * 3),
    )(index, amp, src_index, src_amp)


def advance(p, now, before, before_at, coeff, coeff_at, recv_a, recv_b, added, added_at, out, margin):
    g = lax.axis_index("grp")
    even = lax.rem(g, 2) == 0
    beyond = jnp.where(even, g > 0, g < p.n_grp - 1)
    first = p.base_row() - margin
    count = p.half + 2 * margin
    column = lax.broadcasted_iota(jnp.int32, (8, p.ny), 1)
    line = lax.broadcasted_iota(jnp.int32, (8, p.ny), 0)
    for r in range(0, count, 8):
        rows = slice(r, r + 8)
        weights = [
            [coeff[i * p.lays + lay, coeff_at + r : coeff_at + r + 8, :] for i in range(3)]
            for lay in range(p.lays)
        ]
        edge = r < margin or r + 8 > p.half + margin
        if edge:
            grid_row = first + r + line
            known = (grid_row >= 0) & (grid_row < p.nx)
        for f in range(p.fields):
            far = jnp.where(beyond, recv_b[f, rows, :], 0.0)
            near = recv_a[f, rows, :]
            below = jnp.where(even, far, near)
            above = jnp.where(even, near, far)
            mids = [
                now[f * p.lays + lay, REACH + r : REACH + r + 8, :] for lay in range(p.lays)
            ]
            column_of = [below] + mids + [above]
            for lay in range(p.lays):
                plane = f * p.lays + lay
                x = mids[lay]
                dxx = STENCIL[0] * x
                dyy = STENCIL[0] * x
                for j in range(1, REACH + 1):
                    dxx = dxx + STENCIL[j] * (
                        now[plane, REACH + r + j : REACH + r + j + 8, :]
                        + now[plane, REACH + r - j : REACH + r - j + 8, :]
                    )
                    right = jnp.where(column < p.ny - j, pltpu.roll(x, p.ny - j, 1), 0.0)
                    left = jnp.where(column >= j, pltpu.roll(x, j, 1), 0.0)
                    dyy = dyy + STENCIL[j] * (right + left)
                dzz = column_of[lay] + column_of[lay + 2] - 2.0 * x
                w = weights[lay]
                new = (
                    2.0 * x
                    - before[plane, before_at + r : before_at + r + 8, :]
                    + (w[0] * dxx + w[1] * dyy + w[2] * dzz)
                )
                new = new + added[f, lay, added_at + r : added_at + r + 8, :]
                if edge:
                    new = jnp.where(known, new, 0.0)
                out[plane, rows, :] = new


def first_kernel(
    p, now, recv_a, recv_b, own, other, halo_own, halo_other, added,
    out, coeff_out, send_a, send_b, rest,
):
    lay_out(p, rest, own, other, halo_own, halo_other)
    planes = p.fields * p.lays
    gap = p.d0 - p.d1
    coeff_out[...] = rest[planes:, p.d0 - p.d2 : p.d0 - p.d2 + p.e2, :]
    advance(
        p, now, rest, gap, rest.at[planes:], gap, recv_a, recv_b, added, 0, out, p.d1
    )
    send_layers(p, out, send_a, send_b, p.d1 - p.d2, p.e2)


def first_step(p, now, recv_a, recv_b, rest, added):
    planes = p.fields * p.lays
    return pl.pallas_call(
        functools.partial(first_kernel, p),
        out_shape=(
            f32(planes, p.e1, p.ny),
            f32(3 * p.lays, p.e2, p.ny),
            f32(p.fields, p.e2, p.ny),
            f32(p.fields, p.e2, p.ny),
        ),
        in_specs=[VMEM] * 8,
        out_specs=(VMEM,) * 4,
        scratch_shapes=[pltpu.VMEM((planes + 3 * p.lays, p.e0, p.ny), jnp.float32)],
        compiler_params=PARAMS,
        cost_estimate=cost(60 * planes * p.e1 * p.ny, 8 * planes * p.e1 * p.ny),
    )(now, recv_a, recv_b, *rest, added)


def second_kernel(p, now, before, coeff, recv_a, recv_b, added, out, keep, give):
    gap = p.d1 - p.d2
    advance(
        p, now, before, p.d0 - p.d2, coeff, 0, recv_a, recv_b, added, gap, out, p.d2
    )
    b = lax.axis_index("gy")
    mine = pl.ds(pl.multiple_of(b * p.cols, p.cols), p.cols)
    theirs = pl.ds(pl.multiple_of((1 - b) * p.cols, p.cols), p.cols)
    keep[...] = out[:, p.d2 : p.d2 + p.half, mine]
    give[...] = out[:, p.d2 : p.d2 + p.half, theirs]


def second_step(p, now, before, coeff, recv_a, recv_b, added):
    planes = p.fields * p.lays
    return pl.pallas_call(
        functools.partial(second_kernel, p),
        out_shape=(
            f32(planes, p.e2, p.ny),
            f32(planes, p.half, p.cols),
            f32(planes, p.half, p.cols),
        ),
        in_specs=[VMEM] * 6,
        out_specs=(VMEM,) * 3,
        compiler_params=PARAMS,
        cost_estimate=cost(60 * planes * p.e2 * p.ny, 8 * planes * p.e2 * p.ny),
    )(now, before, coeff, recv_a, recv_b, added)


def image_kernel(p, one, two, offsets, out, held, place, sems):
    for k in range(NOFF):
        place[offsets[k] + MAXOFF] = k
    copies = []
    for d in range(NOFF):
        shift = d - MAXOFF
        for lay in range(p.lays):
            for r in range(0, p.half, 8):
                s1 = one[lay, p.d1 + r : p.d1 + r + 8, :]
                r1 = one[p.lays + lay, p.d1 + r + shift : p.d1 + r + shift + 8, :]
                s2 = two[lay, p.d2 + r : p.d2 + r + 8, :]
                r2 = two[p.lays + lay, p.d2 + r + shift : p.d2 + r + shift + 8, :]
                held[d, lay, r : r + 8, :] = s1 * r1 + s2 * r2
        copy = pltpu.make_async_copy(held.at[d], out.at[place[d]], sems.at[d])
        copy.start()
        copies.append(copy)
    for copy in copies:
        copy.wait()


def correlate_rows(p, one, two, offsets):
    size = NOFF * p.lays * p.half * p.ny
    return pl.pallas_call(
        functools.partial(image_kernel, p),
        out_shape=f32(NOFF, p.lays, p.half, p.ny),
        in_specs=[VMEM] * 2 + [SMEM],
        out_specs=HBM,
        scratch_shapes=[
            pltpu.VMEM((NOFF, p.lays, p.half, p.ny), jnp.float32),
            pltpu.SMEM((NOFF,), jnp.int32),
            pltpu.SemaphoreType.DMA((NOFF,)),
        ],
        compiler_params=PARAMS,
        cost_estimate=cost(3 * size, 4 * size),
    )(one, two, offsets)


def settle_kernel(p, keep, got, out, sems):
    b = lax.axis_index("gy")
    copies = [
        pltpu.make_async_copy(
            source,
            out.at[:, pl.ds(pl.multiple_of(at * p.half, 8), p.half), :],
            sems.at[i],
        )
        for i, (source, at) in enumerate(((keep, b), (got, 1 - b)))
    ]
    for copy in copies:
        copy.start()
    for copy in copies:
        copy.wait()


def settle(p, keep, got):
    planes = p.fields * p.lays
    return pl.pallas_call(
        functools.partial(settle_kernel, p),
        out_shape=f32(planes, p.rows, p.cols),
        in_specs=[VMEM] * 2,
        out_specs=HBM,
        scratch_shapes=[pltpu.SemaphoreType.DMA((2,))],
        compiler_params=PARAMS,
        cost_estimate=cost(0, 8 * planes * p.rows * p.cols),
    )(keep, got)


def pairs_grp(p):
    return [(g, g ^ 1) for g in range(p.n_grp)]


def pairs_between(p):
    pairs = []
    for g in range(p.n_grp):
        to = g + 1 if g % 2 else g - 1
        for a in range(p.n_gx):
            goal = (to, a) if 0 <= to < p.n_grp else (g, a ^ 1)
            pairs.append((g * p.n_gx + a, goal[0] * p.n_gx + goal[1]))
    return pairs


def halo_pairs(p, across):
    size = (p.n_grp, p.n_gx, p.n_gy)

    def flat(place):
        return (place[0] * size[1] + place[1]) * size[2] + place[2]

    goals = {}
    for g in range(p.n_grp):
        for a in range(p.n_gx):
            for b in range(p.n_gy):
                down = (b == 0) != across
                goal = (g, a + 1 if down else a - 1, 1 - b if across else b)
                if 0 <= goal[1] < p.n_gx:
                    goals[(g, a, b)] = goal
    taken = set(goals.values())
    for g in range(p.n_grp):
        for a in range(p.n_gx):
            for b in range(p.n_gy):
                if (g, a, b) not in goals:
                    near = (g ^ 1, a, b) if across else (g, a, 1 - b)
                    assert near not in taken
                    goals[(g, a, b)] = near
    return [(flat(k), flat(v)) for k, v in goals.items()]


AXES = ("grp", "gx", "gy")


def body_rows(p, previous, current, coeff, src_index, src_amp, rec_index, rec_amp, offsets):
    planes = p.fields * p.lays
    tile = (p.rows, p.cols)

    def redistribute(*sources):
        own, give, edge, corner = pack(p, *sources)
        other = lax.ppermute(give, "gy", [(0, 1), (1, 0)])
        halo_own = lax.ppermute(edge, AXES, halo_pairs(p, False))
        halo_other = lax.ppermute(corner, AXES, halo_pairs(p, True))
        return own, other, halo_own, halo_other

    def swap_layers(send_a, send_b):
        recv_a = lax.ppermute(send_a, "grp", pairs_grp(p))
        recv_b = lax.ppermute(send_b, ("grp", "gx"), pairs_between(p))
        return recv_a, recv_b

    count = rec_index.shape[0]
    wide = -(-count // 128)
    if wide * 128 > count:
        rec_index = jnp.pad(rec_index, (0, wide * 128 - count))
        rec_amp = jnp.pad(rec_amp, ((0, 0), (0, wide * 128 - count)))
    points = (rec_index.reshape(wide, 128), rec_amp, src_index, src_amp.reshape(-1))

    now = redistribute(current.reshape(planes, *tile))
    rest = redistribute(previous.reshape(planes, *tile), coeff.reshape(3 * p.lays, *tile))
    added = []
    for step in range(STEPS):
        added.append(spread(p, step, *points))
    whole, send_a, send_b = join(p, *now)
    recv_a, recv_b = swap_layers(send_a, send_b)
    one, weights, send_a, send_b = first_step(p, whole, recv_a, recv_b, rest, added[0])
    recv_a, recv_b = swap_layers(send_a, send_b)
    two, keep, give = second_step(p, one, whole, weights, recv_a, recv_b, added[1])
    got = lax.ppermute(give, "gy", [(0, 1), (1, 0)])
    images = correlate_rows(p, one, two, offsets)
    advanced = settle(p, keep, got)
    return images, advanced.reshape(p.fields, p.lays, *tile)


def solution(mesh):
    planned = mesh.shape["gy"] == 2 and mesh.shape["grp"] % 2 == 0 and mesh.shape["gx"] % 2 == 0

    def body(previous, *others):
        p = Plan(previous.shape, mesh.shape)
        if planned and p.fits():
            return body_rows(p, previous, *others)
        return body_tiles(previous, *others)

    return jax.shard_map(
        body,
        mesh=mesh,
        in_specs=(
            P(None, "grp", "gx", "gy"),
            P(None, "grp", "gx", "gy"),
            P(None, "grp", "gx", "gy"),
            P(),
            P(),
            P(),
            P(),
            P(),
        ),
        out_specs=(P(None, "grp", ("gx", "gy"), None), P(None, "grp", "gx", "gy")),
        check_vma=False,
    )
```

```python
import functools

import jax
import jax.numpy as jnp
from jax import lax
from jax.experimental import pallas as pl
from jax.experimental.pallas import tpu as pltpu
from jax.sharding import PartitionSpec as P


STEPS = 2
NOFF = 17
MAXOFF = 8
REACH = 4


STENCIL = (-205.0 / 72.0, 8.0 / 5.0, -1.0 / 5.0, 8.0 / 315.0, -1.0 / 560.0)


def padded_2(block, sides, width):
    for axis, dim in sides:
        count = lax.axis_size(axis)
        forward = [(i, i + 1) for i in range(count - 1)]
        backward = [(target, source) for source, target in forward]
        low = lax.ppermute(
            lax.slice_in_dim(block, block.shape[dim] - width, None, axis=dim), axis, forward
        )
        high = lax.ppermute(lax.slice_in_dim(block, 0, width, axis=dim), axis, backward)
        block = jnp.concatenate([low, block, high], axis=dim)
    return block


def laplace(cur, coeff):
    wide = padded_2(cur, (("gx", 2), ("gy", 3)), 4)
    deep = padded_2(cur, (("grp", 1),), 1)
    rows = cur.shape[2]
    cols = cur.shape[3]
    dxx = STENCIL[0] * cur
    dyy = STENCIL[0] * cur
    for j in range(1, 5):
        dxx = dxx + STENCIL[j] * (
            wide[:, :, 4 + j : 4 + j + rows, 4 : 4 + cols]
            + wide[:, :, 4 - j : 4 - j + rows, 4 : 4 + cols]
        )
        dyy = dyy + STENCIL[j] * (
            wide[:, :, 4 : 4 + rows, 4 + j : 4 + j + cols]
            + wide[:, :, 4 : 4 + rows, 4 - j : 4 - j + cols]
        )
    dzz = deep[:, 2:] + deep[:, :-2] - 2.0 * cur
    return coeff[0] * dxx + coeff[1] * dyy + coeff[2] * dzz


def inject(field, index, amp):
    layers, rows, cols = field.shape
    total_rows = rows * lax.axis_size("gx")
    total_cols = cols * lax.axis_size("gy")
    layer_at = index // (total_rows * total_cols) - lax.axis_index("grp") * layers
    row_at = index // total_cols % total_rows - lax.axis_index("gx") * rows
    col_at = index % total_cols - lax.axis_index("gy") * cols
    inside = (
        (layer_at >= 0)
        & (layer_at < layers)
        & (row_at >= 0)
        & (row_at < rows)
        & (col_at >= 0)
        & (col_at < cols)
    )
    layer_at = jnp.clip(layer_at, 0, layers - 1)
    row_at = jnp.clip(row_at, 0, rows - 1)
    col_at = jnp.clip(col_at, 0, cols - 1)
    return field.at[layer_at, row_at, col_at].add(jnp.where(inside, amp, 0.0))


def correlate(source, padded, offsets, rows):
    pieces = []
    for k in range(NOFF):
        start = offsets[k] + MAXOFF
        moved = lax.dynamic_slice_in_dim(padded, start, rows, axis=2)
        pieces.append(jnp.sum(source * moved, axis=0))
    return jnp.stack(pieces)


def body_tiles(previous, current, coeff, src_index, src_amp, rec_index, rec_amp, offsets):
    prev, cur = (previous, current)
    snapshots = []
    for step in range(STEPS):
        nxt = 2.0 * cur - prev + laplace(cur, coeff)
        src_field = inject(nxt[0], src_index, src_amp[step])
        rec_field = inject(nxt[1], rec_index, rec_amp[step])
        nxt = jnp.stack([src_field, rec_field])
        snapshots.append(nxt)
        prev, cur = (cur, nxt)
    snaps = jnp.stack(snapshots)
    moved = lax.all_to_all(snaps, "gy", split_axis=3, concat_axis=4, tiled=True)
    source = moved[:, 0]
    padded = padded_2(moved[:, 1], ((("gx", "gy"), 2),), MAXOFF)
    images = correlate(source, padded, offsets, source.shape[2])
    return (images, cur)


VMEM = pl.BlockSpec(memory_space=pltpu.VMEM)
HBM = pl.BlockSpec(memory_space=pltpu.HBM)
EARLY = 6
PARAMS = pltpu.CompilerParams(vmem_limit_bytes=16 << 20)


class Plan:
    def __init__(self, shape, mesh_shape):
        self.fields, self.lays, self.rows, self.cols = shape
        self.n_grp, self.n_gx, self.n_gy = (mesh_shape[k] for k in ("grp", "gx", "gy"))
        self.nx = self.rows * self.n_gx
        self.ny = self.cols * self.n_gy
        self.half = self.rows // self.n_gy
        self.d2 = MAXOFF
        self.d1 = MAXOFF + REACH
        self.d0 = MAXOFF + 2 * REACH
        self.inside = self.half + self.d0
        self.e0 = self.half + 2 * self.d0
        self.e1 = self.half + 2 * self.d1
        self.e2 = self.half + 2 * self.d2

    def fits(self):
        return (
            self.n_gy == 2
            and self.n_grp % 2 == 0
            and self.n_gx % 2 == 0
            and self.rows % 16 == 0
            and self.cols % 128 == 0
            and self.inside <= self.rows
            and STEPS == 2
        )

    def base_row(self):
        return lax.axis_index("gx") * self.rows + lax.axis_index("gy") * self.half


def cost(flops, moved):
    return pl.CostEstimate(flops=flops, bytes_accessed=moved, transcendentals=0)


def f32(*shape):
    return jax.ShapeDtypeStruct(shape, jnp.float32)


def pack_kernel(p, groups, extra, *refs):
    refs = list(refs)

    def take(n):
        taken = refs[:n]
        del refs[:n]
        return taken

    sources = [take(n) for n in groups]
    smalls = take(extra)
    outs = [take(4) for _ in groups]
    held = take(extra)
    sems, small_sems = refs
    b = lax.axis_index("gy")
    starts = (
        ((1 - b) * (p.rows - p.inside), p.inside),
        (b * (p.rows - p.inside), p.inside),
        ((1 - b) * (p.rows - p.d0), p.d0),
        (b * (p.rows - p.d0), p.d0),
    )
    targets = (1, 0, 2, 3)
    copies = []
    i = 0
    for members, out in zip(sources, outs):
        plane = 0
        for source in members:
            planes = source.shape[0]
            for j, (start, size) in zip(targets, starts):
                copies.append(
                    pltpu.make_async_copy(
                        source.at[:, pl.ds(pl.multiple_of(start, 8), size), :],
                        out[j].at[pl.ds(plane, planes)],
                        sems.at[i, j],
                    )
                )
            plane += planes
            i += 1
    for i in range(extra):
        copies.append(pltpu.make_async_copy(smalls[i], held[i], small_sems.at[i]))
    for copy in copies:
        copy.start()
    for copy in copies:
        copy.wait()


def in_hbm(x):
    return pltpu.with_memory_space_constraint(x, pltpu.HBM)


def pack(p, groups, smalls):
    flat = [x for group in groups for x in group]
    shapes = []
    for group in groups:
        planes = sum(x.shape[0] for x in group)
        shapes += [f32(planes, size, p.cols) for size in (p.inside, p.inside, p.d0, p.d0)]
    shapes += [jax.ShapeDtypeStruct(x.shape, x.dtype) for x in smalls]
    outs = pl.pallas_call(
        functools.partial(pack_kernel, p, [len(group) for group in groups], len(smalls)),
        out_shape=tuple(shapes),
        in_specs=[HBM] * (len(flat) + len(smalls)),
        out_specs=(VMEM,) * len(shapes),
        scratch_shapes=[
            pltpu.SemaphoreType.DMA((len(flat), 4)),
            pltpu.SemaphoreType.DMA((max(1, len(smalls)),)),
        ],
        compiler_params=PARAMS,
        cost_estimate=cost(0, 4 * sum(x.size for x in flat) * 3),
    )(*(in_hbm(x) for x in (*flat, *smalls)))
    count = 4 * len(groups)
    return [outs[i : i + 4] for i in range(0, count, 4)], outs[count:]


def lay_out(p, target, own, other, halo_own, halo_other):
    a = lax.axis_index("gx")
    b = lax.axis_index("gy")
    mine = pl.ds(pl.multiple_of(b * p.cols, p.cols), p.cols)
    theirs = pl.ds(pl.multiple_of((1 - b) * p.cols, p.cols), p.cols)
    inner = pl.ds(pl.multiple_of((1 - b) * p.d0, 8), p.inside)
    outer = pl.ds(pl.multiple_of(b * p.inside, 8), p.d0)
    there = jnp.where(b == 0, a > 0, a < p.n_gx - 1)
    target[:, inner, mine] = own[...]
    target[:, inner, theirs] = other[...]
    target[:, outer, mine] = jnp.where(there, halo_own[...], 0.0)
    target[:, outer, theirs] = jnp.where(there, halo_other[...], 0.0)


def send_layers(p, whole, send_a, send_b, shift, count):
    odd = lax.rem(lax.axis_index("grp"), 2)
    lay_a = (1 - odd) * (p.lays - 1)
    lay_b = odd * (p.lays - 1)
    for f in range(p.fields):
        send_a[f] = whole[f * p.lays + lay_a, shift : shift + count, :]
        send_b[f] = whole[f * p.lays + lay_b, shift : shift + count, :]


def join_kernel(p, own, other, halo_own, halo_other, whole, send_a, send_b):
    lay_out(p, whole, own, other, halo_own, halo_other)
    send_layers(p, whole, send_a, send_b, p.d0 - p.d1, p.e1)


def join(p, own, other, halo_own, halo_other):
    planes = own.shape[0]
    return pl.pallas_call(
        functools.partial(join_kernel, p),
        out_shape=(
            f32(planes, p.e0, p.ny),
            f32(p.fields, p.e1, p.ny),
            f32(p.fields, p.e1, p.ny),
        ),
        in_specs=[VMEM] * 4,
        out_specs=(VMEM,) * 3,
        compiler_params=PARAMS,
        cost_estimate=cost(0, 8 * planes * p.e0 * p.ny),
    )(own, other, halo_own, halo_other)


def spread_kernel(
    p, step, index, amp, src_index_in, src_amp_in,
    out, row_hot, col_hot, total, src_index, src_amp, sems,
):
    fetches = [
        pltpu.make_async_copy(src_index_in, src_index, sems.at[0]),
        pltpu.make_async_copy(src_amp_in, src_amp, sems.at[1]),
    ]
    for fetch in fetches:
        fetch.start()
    lays, stride = p.lays, p.e0
    g = lax.axis_index("grp")
    first = p.base_row() - p.d1
    wide = index.shape[0]
    grid_row = first + lax.broadcasted_iota(jnp.int32, (stride, 128), 0)
    known = (grid_row >= 0) & (grid_row < p.nx)
    wanted = [
        jnp.where(known, (g * lays + lay) * p.nx + grid_row, -1) for lay in range(lays)
    ]
    column = lax.broadcasted_iota(jnp.int32, (p.ny, 128), 0)
    for k in range(wide):
        at = slice(k * 128, (k + 1) * 128)
        flat = index[k : k + 1, :]
        row = jnp.floor((flat.astype(jnp.float32) + 0.5) * (1.0 / p.ny)).astype(jnp.int32)
        col = flat - row * p.ny
        col_hot[:, at] = jnp.where(column == col, 1.0, 0.0).astype(jnp.bfloat16)
        rest = amp[step : step + 1, at]
        parts = []
        for _ in range(3):
            part = rest.astype(jnp.bfloat16).astype(jnp.float32)
            parts.append(part)
            rest = rest - part
        for lay in range(lays):
            hit = wanted[lay] == row
            for i, part in enumerate(parts):
                start = (i * lays + lay) * stride
                row_hot[start : start + stride, at] = jnp.where(hit, part, 0.0).astype(
                    jnp.bfloat16
                )
    total[...] = lax.dot_general(
        row_hot[...],
        col_hot[...],
        (((1,), (1,)), ((), ())),
        preferred_element_type=jnp.float32,
    )
    for lay in range(lays):
        rows = [(i * lays + lay) * stride for i in range(3)]
        out[1, lay] = (
            total[rows[0] : rows[0] + p.e1]
            + total[rows[1] : rows[1] + p.e1]
            + total[rows[2] : rows[2] + p.e1]
        )
    out[0] = jnp.zeros((lays, p.e1, p.ny), jnp.float32)
    for fetch in fetches:
        fetch.wait()
    for s in range(src_index.shape[0]):
        flat = src_index[s]
        line = lax.div(flat, p.ny)
        lay = lax.div(line, p.nx) - g * lays
        row = lax.rem(line, p.nx) - first
        col = lax.rem(flat, p.ny)

        @pl.when((lay >= 0) & (lay < lays) & (row >= 0) & (row < p.e1))
        def _():
            spot = lax.broadcasted_iota(jnp.int32, (1, p.ny), 1) == col
            out[0, lay, pl.ds(row, 1), :] += jnp.where(spot, src_amp[s, step], 0.0)


def spread(p, step, index, amp, src_index, src_amp):
    wide = index.shape[0]
    tall = 3 * p.lays * p.e0
    return pl.pallas_call(
        functools.partial(spread_kernel, p, step),
        out_shape=f32(p.fields, p.lays, p.e1, p.ny),
        in_specs=[VMEM] * 2 + [HBM] * 2,
        out_specs=VMEM,
        scratch_shapes=[
            pltpu.VMEM((tall, wide * 128), jnp.bfloat16),
            pltpu.VMEM((p.ny, wide * 128), jnp.bfloat16),
            pltpu.VMEM((tall, p.ny), jnp.float32),
            pltpu.SMEM(src_index.shape, jnp.int32),
            pltpu.SMEM(src_amp.shape, jnp.float32),
            pltpu.SemaphoreType.DMA((2,)),
        ],
        compiler_params=PARAMS,
        cost_estimate=cost(2 * tall * wide * 128 * p.ny, 4 * wide * 128 * 3),
    )(index, amp, src_index, in_hbm(src_amp))


def advance(p, now, before, before_at, coeff, coeff_at, recv_a, recv_b, added, added_at, out, margin):
    g = lax.axis_index("grp")
    even = lax.rem(g, 2) == 0
    beyond = jnp.where(even, g > 0, g < p.n_grp - 1)
    first = p.base_row() - margin
    count = p.half + 2 * margin
    column = lax.broadcasted_iota(jnp.int32, (8, p.ny), 1)
    line = lax.broadcasted_iota(jnp.int32, (8, p.ny), 0)
    for r in range(0, count, 8):
        rows = slice(r, r + 8)
        weights = [
            [coeff[i * p.lays + lay, coeff_at + r : coeff_at + r + 8, :] for i in range(3)]
            for lay in range(p.lays)
        ]
        edge = r < margin or r + 8 > p.half + margin
        if edge:
            grid_row = first + r + line
            known = (grid_row >= 0) & (grid_row < p.nx)
        for f in range(p.fields):
            far = jnp.where(beyond, recv_b[f, rows, :], 0.0)
            near = recv_a[f, rows, :]
            below = jnp.where(even, far, near)
            above = jnp.where(even, near, far)
            mids = [
                now[f * p.lays + lay, REACH + r : REACH + r + 8, :] for lay in range(p.lays)
            ]
            column_of = [below] + mids + [above]
            for lay in range(p.lays):
                plane = f * p.lays + lay
                x = mids[lay]
                dxx = STENCIL[0] * x
                dyy = STENCIL[0] * x
                for j in range(1, REACH + 1):
                    dxx = dxx + STENCIL[j] * (
                        now[plane, REACH + r + j : REACH + r + j + 8, :]
                        + now[plane, REACH + r - j : REACH + r - j + 8, :]
                    )
                    right = jnp.where(column < p.ny - j, pltpu.roll(x, p.ny - j, 1), 0.0)
                    left = jnp.where(column >= j, pltpu.roll(x, j, 1), 0.0)
                    dyy = dyy + STENCIL[j] * (right + left)
                dzz = column_of[lay] + column_of[lay + 2] - 2.0 * x
                w = weights[lay]
                new = (
                    2.0 * x
                    - before[plane, before_at + r : before_at + r + 8, :]
                    + (w[0] * dxx + w[1] * dyy + w[2] * dzz)
                )
                new = new + added[f, lay, added_at + r : added_at + r + 8, :]
                if edge:
                    new = jnp.where(known, new, 0.0)
                out[plane, rows, :] = new


def first_kernel(
    p, now, recv_a, recv_b, own, other, halo_own, halo_other, added,
    out, coeff_out, send_a, send_b, rest,
):
    lay_out(p, rest, own, other, halo_own, halo_other)
    planes = p.fields * p.lays
    gap = p.d0 - p.d1
    coeff_out[...] = rest[planes:, p.d0 - p.d2 : p.d0 - p.d2 + p.e2, :]
    advance(
        p, now, rest, gap, rest.at[planes:], gap, recv_a, recv_b, added, 0, out, p.d1
    )
    send_layers(p, out, send_a, send_b, p.d1 - p.d2, p.e2)


def first_step(p, now, recv_a, recv_b, rest, added):
    planes = p.fields * p.lays
    return pl.pallas_call(
        functools.partial(first_kernel, p),
        out_shape=(
            f32(planes, p.e1, p.ny),
            f32(3 * p.lays, p.e2, p.ny),
            f32(p.fields, p.e2, p.ny),
            f32(p.fields, p.e2, p.ny),
        ),
        in_specs=[VMEM] * 8,
        out_specs=(VMEM,) * 4,
        scratch_shapes=[pltpu.VMEM((planes + 3 * p.lays, p.e0, p.ny), jnp.float32)],
        compiler_params=PARAMS,
        cost_estimate=cost(60 * planes * p.e1 * p.ny, 8 * planes * p.e1 * p.ny),
    )(now, recv_a, recv_b, *rest, added)


def second_kernel(p, now, before, coeff, recv_a, recv_b, added, out, keep, give):
    gap = p.d1 - p.d2
    advance(
        p, now, before, p.d0 - p.d2, coeff, 0, recv_a, recv_b, added, gap, out, p.d2
    )
    b = lax.axis_index("gy")
    mine = pl.ds(pl.multiple_of(b * p.cols, p.cols), p.cols)
    theirs = pl.ds(pl.multiple_of((1 - b) * p.cols, p.cols), p.cols)
    keep[...] = out[:, p.d2 : p.d2 + p.half, mine]
    give[...] = out[:, p.d2 : p.d2 + p.half, theirs]


def second_step(p, now, before, coeff, recv_a, recv_b, added):
    planes = p.fields * p.lays
    return pl.pallas_call(
        functools.partial(second_kernel, p),
        out_shape=(
            f32(planes, p.e2, p.ny),
            f32(planes, p.half, p.cols),
            f32(planes, p.half, p.cols),
        ),
        in_specs=[VMEM] * 6,
        out_specs=(VMEM,) * 3,
        compiler_params=PARAMS,
        cost_estimate=cost(60 * planes * p.e2 * p.ny, 8 * planes * p.e2 * p.ny),
    )(now, before, coeff, recv_a, recv_b, added)


def image_kernel(p, one, two, offsets, out, held, order, place, sems, order_sem):
    fetch = pltpu.make_async_copy(offsets, order, order_sem)
    fetch.start()
    copies = []
    ready = 0

    def launch(d):
        copy = pltpu.make_async_copy(held.at[d], out.at[place[d]], sems.at[d])
        copy.start()
        copies.append(copy)

    for d in range(NOFF):
        shift = d - MAXOFF
        for lay in range(p.lays):
            for r in range(0, p.half, 8):
                s1 = one[lay, p.d1 + r : p.d1 + r + 8, :]
                r1 = one[p.lays + lay, p.d1 + r + shift : p.d1 + r + shift + 8, :]
                s2 = two[lay, p.d2 + r : p.d2 + r + 8, :]
                r2 = two[p.lays + lay, p.d2 + r + shift : p.d2 + r + shift + 8, :]
                held[d, lay, r : r + 8, :] = s1 * r1 + s2 * r2
        if d < EARLY:
            continue
        if d == EARLY:
            fetch.wait()
            for k in range(NOFF):
                place[order[k] + MAXOFF] = k
        while ready <= d:
            launch(ready)
            ready += 1
    for copy in copies:
        copy.wait()


def correlate_rows(p, one, two, offsets):
    size = NOFF * p.lays * p.half * p.ny
    return pl.pallas_call(
        functools.partial(image_kernel, p),
        out_shape=f32(NOFF, p.lays, p.half, p.ny),
        in_specs=[VMEM] * 2 + [HBM],
        out_specs=HBM,
        scratch_shapes=[
            pltpu.VMEM((NOFF, p.lays, p.half, p.ny), jnp.float32),
            pltpu.SMEM((NOFF,), jnp.int32),
            pltpu.SMEM((NOFF,), jnp.int32),
            pltpu.SemaphoreType.DMA((NOFF,)),
            pltpu.SemaphoreType.DMA,
        ],
        compiler_params=PARAMS,
        cost_estimate=cost(3 * size, 4 * size),
    )(one, two, in_hbm(offsets))


def settle_kernel(p, keep, got, out, sems):
    b = lax.axis_index("gy")
    copies = [
        pltpu.make_async_copy(
            source,
            out.at[:, pl.ds(pl.multiple_of(at * p.half, 8), p.half), :],
            sems.at[i],
        )
        for i, (source, at) in enumerate(((keep, b), (got, 1 - b)))
    ]
    for copy in copies:
        copy.start()
    for copy in copies:
        copy.wait()


def settle(p, keep, got):
    planes = p.fields * p.lays
    return pl.pallas_call(
        functools.partial(settle_kernel, p),
        out_shape=f32(planes, p.rows, p.cols),
        in_specs=[VMEM] * 2,
        out_specs=HBM,
        scratch_shapes=[pltpu.SemaphoreType.DMA((2,))],
        compiler_params=PARAMS,
        cost_estimate=cost(0, 8 * planes * p.rows * p.cols),
    )(keep, got)


def pairs_grp(p):
    return [(g, g ^ 1) for g in range(p.n_grp)]


def pairs_between(p):
    pairs = []
    for g in range(p.n_grp):
        to = g + 1 if g % 2 else g - 1
        for a in range(p.n_gx):
            goal = (to, a) if 0 <= to < p.n_grp else (g, a ^ 1)
            pairs.append((g * p.n_gx + a, goal[0] * p.n_gx + goal[1]))
    return pairs


def halo_pairs(p, across):
    size = (p.n_grp, p.n_gx, p.n_gy)

    def flat(place):
        return (place[0] * size[1] + place[1]) * size[2] + place[2]

    goals = {}
    for g in range(p.n_grp):
        for a in range(p.n_gx):
            for b in range(p.n_gy):
                down = (b == 0) != across
                goal = (g, a + 1 if down else a - 1, 1 - b if across else b)
                if 0 <= goal[1] < p.n_gx:
                    goals[(g, a, b)] = goal
    taken = set(goals.values())
    for g in range(p.n_grp):
        for a in range(p.n_gx):
            for b in range(p.n_gy):
                if (g, a, b) not in goals:
                    near = (g ^ 1, a, b) if across else (g, a, 1 - b)
                    assert near not in taken
                    goals[(g, a, b)] = near
    return [(flat(k), flat(v)) for k, v in goals.items()]


AXES = ("grp", "gx", "gy")


def body_rows(p, previous, current, coeff, src_index, src_amp, rec_index, rec_amp, offsets):
    planes = p.fields * p.lays
    tile = (p.rows, p.cols)

    def redistribute(own, give, edge, corner):
        other = lax.ppermute(give, "gy", [(0, 1), (1, 0)])
        halo_own = lax.ppermute(edge, AXES, halo_pairs(p, False))
        halo_other = lax.ppermute(corner, AXES, halo_pairs(p, True))
        return own, other, halo_own, halo_other

    def swap_layers(send_a, send_b):
        recv_a = lax.ppermute(send_a, "grp", pairs_grp(p))
        recv_b = lax.ppermute(send_b, ("grp", "gx"), pairs_between(p))
        return recv_a, recv_b

    count = rec_index.shape[0]
    wide = -(-count // 128)
    if wide * 128 > count:
        rec_index = jnp.pad(rec_index, (0, wide * 128 - count))
        rec_amp = jnp.pad(rec_amp, ((0, 0), (0, wide * 128 - count)))
    points = (rec_index.reshape(wide, 128), rec_amp)

    (now, rest), points = pack(
        p,
        (
            (current.reshape(planes, *tile),),
            (previous.reshape(planes, *tile), coeff.reshape(3 * p.lays, *tile)),
        ),
        points,
    )
    now = redistribute(*now)
    rest = redistribute(*rest)
    added = []
    for step in range(STEPS):
        added.append(spread(p, step, *points, src_index, src_amp.T))
    whole, send_a, send_b = join(p, *now)
    recv_a, recv_b = swap_layers(send_a, send_b)
    one, weights, send_a, send_b = first_step(p, whole, recv_a, recv_b, rest, added[0])
    recv_a, recv_b = swap_layers(send_a, send_b)
    two, keep, give = second_step(p, one, whole, weights, recv_a, recv_b, added[1])
    got = lax.ppermute(give, "gy", [(0, 1), (1, 0)])
    images = correlate_rows(p, one, two, offsets)
    advanced = settle(p, keep, got)
    return images, advanced.reshape(p.fields, p.lays, *tile)


def solution(mesh):
    planned = mesh.shape["gy"] == 2 and mesh.shape["grp"] % 2 == 0 and mesh.shape["gx"] % 2 == 0

    def body(previous, *others):
        p = Plan(previous.shape, mesh.shape)
        if planned and p.fits():
            return body_rows(p, previous, *others)
        return body_tiles(previous, *others)

    return jax.shard_map(
        body,
        mesh=mesh,
        in_specs=(
            P(None, "grp", "gx", "gy"),
            P(None, "grp", "gx", "gy"),
            P(None, "grp", "gx", "gy"),
            P(),
            P(),
            P(),
            P(),
            P(),
        ),
        out_specs=(P(None, "grp", ("gx", "gy"), None), P(None, "grp", "gx", "gy")),
        check_vma=False,
    )
```

```python
import functools

import jax
import jax.numpy as jnp
from jax import lax
from jax.experimental import pallas as pl
from jax.experimental.pallas import tpu as pltpu
from jax.sharding import PartitionSpec as P


STEPS = 2
NOFF = 17
MAXOFF = 8
REACH = 4


STENCIL = (-205.0 / 72.0, 8.0 / 5.0, -1.0 / 5.0, 8.0 / 315.0, -1.0 / 560.0)


def padded_2(block, sides, width):
    for axis, dim in sides:
        count = lax.axis_size(axis)
        forward = [(i, i + 1) for i in range(count - 1)]
        backward = [(target, source) for source, target in forward]
        low = lax.ppermute(
            lax.slice_in_dim(block, block.shape[dim] - width, None, axis=dim), axis, forward
        )
        high = lax.ppermute(lax.slice_in_dim(block, 0, width, axis=dim), axis, backward)
        block = jnp.concatenate([low, block, high], axis=dim)
    return block


def laplace(cur, coeff):
    wide = padded_2(cur, (("gx", 2), ("gy", 3)), 4)
    deep = padded_2(cur, (("grp", 1),), 1)
    rows = cur.shape[2]
    cols = cur.shape[3]
    dxx = STENCIL[0] * cur
    dyy = STENCIL[0] * cur
    for j in range(1, 5):
        dxx = dxx + STENCIL[j] * (
            wide[:, :, 4 + j : 4 + j + rows, 4 : 4 + cols]
            + wide[:, :, 4 - j : 4 - j + rows, 4 : 4 + cols]
        )
        dyy = dyy + STENCIL[j] * (
            wide[:, :, 4 : 4 + rows, 4 + j : 4 + j + cols]
            + wide[:, :, 4 : 4 + rows, 4 - j : 4 - j + cols]
        )
    dzz = deep[:, 2:] + deep[:, :-2] - 2.0 * cur
    return coeff[0] * dxx + coeff[1] * dyy + coeff[2] * dzz


def inject(field, index, amp):
    layers, rows, cols = field.shape
    total_rows = rows * lax.axis_size("gx")
    total_cols = cols * lax.axis_size("gy")
    layer_at = index // (total_rows * total_cols) - lax.axis_index("grp") * layers
    row_at = index // total_cols % total_rows - lax.axis_index("gx") * rows
    col_at = index % total_cols - lax.axis_index("gy") * cols
    inside = (
        (layer_at >= 0)
        & (layer_at < layers)
        & (row_at >= 0)
        & (row_at < rows)
        & (col_at >= 0)
        & (col_at < cols)
    )
    layer_at = jnp.clip(layer_at, 0, layers - 1)
    row_at = jnp.clip(row_at, 0, rows - 1)
    col_at = jnp.clip(col_at, 0, cols - 1)
    return field.at[layer_at, row_at, col_at].add(jnp.where(inside, amp, 0.0))


def correlate(source, padded, offsets, rows):
    pieces = []
    for k in range(NOFF):
        start = offsets[k] + MAXOFF
        moved = lax.dynamic_slice_in_dim(padded, start, rows, axis=2)
        pieces.append(jnp.sum(source * moved, axis=0))
    return jnp.stack(pieces)


def body_tiles(previous, current, coeff, src_index, src_amp, rec_index, rec_amp, offsets):
    prev, cur = (previous, current)
    snapshots = []
    for step in range(STEPS):
        nxt = 2.0 * cur - prev + laplace(cur, coeff)
        src_field = inject(nxt[0], src_index, src_amp[step])
        rec_field = inject(nxt[1], rec_index, rec_amp[step])
        nxt = jnp.stack([src_field, rec_field])
        snapshots.append(nxt)
        prev, cur = (cur, nxt)
    snaps = jnp.stack(snapshots)
    moved = lax.all_to_all(snaps, "gy", split_axis=3, concat_axis=4, tiled=True)
    source = moved[:, 0]
    padded = padded_2(moved[:, 1], ((("gx", "gy"), 2),), MAXOFF)
    images = correlate(source, padded, offsets, source.shape[2])
    return (images, cur)


VMEM = pl.BlockSpec(memory_space=pltpu.VMEM)
HBM = pl.BlockSpec(memory_space=pltpu.HBM)
EARLY = 6
PARAMS = pltpu.CompilerParams(vmem_limit_bytes=16 << 20)


class Plan:
    def __init__(self, shape, mesh_shape):
        self.fields, self.lays, self.rows, self.cols = shape
        self.n_grp, self.n_gx, self.n_gy = (mesh_shape[k] for k in ("grp", "gx", "gy"))
        self.nx = self.rows * self.n_gx
        self.ny = self.cols * self.n_gy
        self.planes = self.fields * self.lays
        self.half = self.rows // self.n_gy
        self.d2 = MAXOFF
        self.d1 = MAXOFF + REACH
        self.d0 = MAXOFF + 2 * REACH
        self.e0 = self.rows + 2 * self.d0
        self.e1 = self.rows + 2 * self.d1
        self.e2 = self.rows + 2 * self.d2
        self.near = self.half + 2 * MAXOFF
        self.lot = self.planes * REACH
        self.lots = self.cols // self.lot
        self.gift = self.lays * (self.half + self.near)

    def fits(self):
        return (
            self.n_gy == 2
            and self.n_grp % 2 == 0
            and self.n_gx % 2 == 0
            and self.rows % 16 == 0
            and self.d0 <= self.rows
            and self.cols == 128
            and self.fields == 2
            and self.lays * self.cols <= 256
            and self.e0 <= 256
            and self.cols % self.lot == 0
            and STEPS == 2
        )


def cost(flops, moved):
    return pl.CostEstimate(flops=flops, bytes_accessed=moved, transcendentals=0)


def f32(*shape):
    return jax.ShapeDtypeStruct(shape, jnp.float32)


def in_hbm(x):
    return pltpu.with_memory_space_constraint(x, pltpu.HBM)


def parity(name):
    return lax.rem(lax.axis_index(name), 2)


def pack_kernel(p, groups, extra, *refs):
    refs = list(refs)

    def take(n):
        taken = refs[:n]
        del refs[:n]
        return taken

    sources = [take(n) for n in groups]
    smalls = take(extra)
    outs = [take(3) for _ in groups]
    held = take(extra)
    sems, small_sems = refs
    odd = parity("gx")
    starts = (
        ((1 - odd) * (p.rows - p.d0), p.d0),
        (odd * (p.rows - p.d0), p.d0),
        (0, p.rows),
    )
    copies = []
    i = 0
    for members, out in zip(sources, outs):
        plane = 0
        for source in members:
            planes = source.shape[0]
            for j, (start, size) in enumerate(starts):
                copies.append(
                    pltpu.make_async_copy(
                        source.at[:, pl.ds(pl.multiple_of(start, 8), size), :],
                        out[j].at[pl.ds(plane, planes)],
                        sems.at[i, j],
                    )
                )
            plane += planes
            i += 1
    for i in range(extra):
        copies.append(pltpu.make_async_copy(smalls[i], held[i], small_sems.at[i]))
    for copy in copies:
        copy.start()
    for copy in copies:
        copy.wait()


def pack(p, groups, smalls):
    flat = [x for group in groups for x in group]
    shapes = []
    for group in groups:
        planes = sum(x.shape[0] for x in group)
        shapes += [f32(planes, size, p.cols) for size in (p.d0, p.d0, p.rows)]
    shapes += [jax.ShapeDtypeStruct(x.shape, x.dtype) for x in smalls]
    outs = pl.pallas_call(
        functools.partial(pack_kernel, p, [len(group) for group in groups], len(smalls)),
        out_shape=tuple(shapes),
        in_specs=[HBM] * (len(flat) + len(smalls)),
        out_specs=(VMEM,) * len(shapes),
        scratch_shapes=[
            pltpu.SemaphoreType.DMA((len(flat), 3)),
            pltpu.SemaphoreType.DMA((max(1, len(smalls)),)),
        ],
        compiler_params=PARAMS,
        cost_estimate=cost(0, 4 * sum(x.size for x in flat) * 3),
    )(*(in_hbm(x) for x in (*flat, *smalls)))
    count = 3 * len(groups)
    return [outs[i : i + 3] for i in range(0, count, 3)], outs[count:]


def lot_rows(p, count):
    return -(-count // (8 * p.lots)) * 8


def lay_out(p, target, own, got_a, got_b):
    a = lax.axis_index("gx")
    odd = parity("gx")
    upper = pl.ds(0, p.d0)
    lower = pl.ds(p.d0 + p.rows, p.d0)
    target[:, p.d0 : p.d0 + p.rows, :] = own[...]

    @pl.when(odd == 0)
    def _():
        target[:, lower, :] = got_a[...]
        target[:, upper, :] = jnp.where(a > 0, got_b[...], 0.0)

    @pl.when(odd == 1)
    def _():
        target[:, upper, :] = got_a[...]
        target[:, lower, :] = jnp.where(a < p.n_gx - 1, got_b[...], 0.0)


def send_edges(p, whole, send_x, send_a, send_b, shift, count):
    odd = parity("grp")
    lay_a = (1 - odd) * (p.lays - 1)
    lay_b = odd * (p.lays - 1)
    for f in range(p.fields):
        send_a[f] = whole[f * p.lays + lay_a, shift : shift + count, :]
        send_b[f] = whole[f * p.lays + lay_b, shift : shift + count, :]
    b = lax.axis_index("gy")
    tall = lot_rows(p, count)
    lane = lax.broadcasted_iota(jnp.int32, (8, p.cols), 1)

    def packed(first):
        for r in range(0, tall, 8):
            block = jnp.zeros((8, p.cols), jnp.float32)
            for lot in range(p.lots):
                row = lot * tall + r
                if row >= count:
                    continue
                for plane in range(p.planes):
                    at = lot * p.lot + plane * REACH
                    moved = (at - first) % p.cols
                    x = whole[plane, shift + row : shift + row + 8, :]
                    x = pltpu.roll(x, moved, 1) if moved else x
                    block = jnp.where((lane >= at) & (lane < at + REACH), x, block)
            send_x[r : r + 8, :] = block

    @pl.when(b == 0)
    def _():
        packed(p.cols - REACH)

    @pl.when(b == 1)
    def _():
        packed(0)


def join_kernel(p, own, got_a, got_b, whole, send_x, send_a, send_b):
    lay_out(p, whole, own, got_a, got_b)
    send_edges(p, whole, send_x, send_a, send_b, p.d0 - p.d1, p.e1)


def edges_shape(p, count):
    return (f32(lot_rows(p, count), p.cols), f32(p.fields, count, p.cols), f32(p.fields, count, p.cols))


def join(p, own, got_a, got_b):
    return pl.pallas_call(
        functools.partial(join_kernel, p),
        out_shape=(f32(p.planes, p.e0, p.cols), *edges_shape(p, p.e1)),
        in_specs=[VMEM] * 3,
        out_specs=(VMEM,) * 4,
        compiler_params=PARAMS,
        cost_estimate=cost(0, 8 * p.planes * p.e0 * p.cols),
    )(own, got_a, got_b)


def whole_part(x, divisor):
    return jnp.floor((x.astype(jnp.float32) + 0.5) * (1.0 / divisor)).astype(jnp.int32)


def mark_kernel(
    p, index, amp, src_index_in, src_amp_in, row_hot, col_hot, source, src_index, src_amp, sems
):
    fetches = [
        pltpu.make_async_copy(src_index_in, src_index, sems.at[0]),
        pltpu.make_async_copy(src_amp_in, src_amp, sems.at[1]),
    ]
    for fetch in fetches:
        fetch.start()
    lays, stride = p.lays, p.e0
    first_lay = lax.axis_index("grp") * lays
    first_row = lax.axis_index("gx") * p.rows - p.d1
    first_col = lax.axis_index("gy") * p.cols
    narrow = jnp.bfloat16
    one, zero = jnp.ones((), narrow), jnp.zeros((), narrow)
    tall = lax.broadcasted_iota(jnp.int32, (stride, 128), 0).astype(jnp.float32).astype(narrow)
    spot = lax.broadcasted_iota(jnp.int32, (lays * p.cols, 128), 0)
    spot = spot.astype(jnp.float32).astype(narrow)

    def whole_number(x, count):
        return jnp.where((x >= 0) & (x < count), x, -1).astype(jnp.float32).astype(narrow)

    for k in range(index.shape[0]):
        at = slice(k * 128, (k + 1) * 128)
        flat = index[k : k + 1, :]
        line = whole_part(flat, p.ny)
        lay = whole_part(line, p.nx)
        row = line - lay * p.nx - first_row
        col = flat - line * p.ny - first_col
        inside = (col >= 0) & (col < p.cols)
        place = whole_number(
            jnp.where(inside, (lay - first_lay) * p.cols + col, -1), lays * p.cols
        )
        col_hot[:, at] = jnp.where(spot == place, one, zero)
        hit = tall == whole_number(row, p.e1)
        for step in range(STEPS):
            rest = amp[step : step + 1, at]
            for i in range(3):
                part = rest.astype(narrow)
                row_hot[step, i * stride : (i + 1) * stride, at] = jnp.where(hit, part, zero)
                rest = rest - part.astype(jnp.float32)
    source[...] = jnp.zeros((STEPS, lays, p.e1, p.cols), jnp.float32)
    for fetch in fetches:
        fetch.wait()
    for s in range(src_index.shape[0]):
        flat = src_index[s]
        line = lax.div(flat, p.ny)
        lay = lax.div(line, p.nx) - first_lay
        row = lax.rem(line, p.nx) - first_row
        col = lax.rem(flat, p.ny) - first_col

        @pl.when((lay >= 0) & (lay < lays) & (row >= 0) & (row < p.e1))
        def _():
            hit = lax.broadcasted_iota(jnp.int32, (1, p.cols), 1) == col
            for step in range(STEPS):
                source[step, lay, pl.ds(row, 1), :] += jnp.where(hit, src_amp[s, step], 0.0)


def mark(p, index, amp, src_index, src_amp):
    wide = index.shape[0] * 128
    return pl.pallas_call(
        functools.partial(mark_kernel, p),
        out_shape=(
            jax.ShapeDtypeStruct((STEPS, 3 * p.e0, wide), jnp.bfloat16),
            jax.ShapeDtypeStruct((p.lays * p.cols, wide), jnp.bfloat16),
            f32(STEPS, p.lays, p.e1, p.cols),
        ),
        in_specs=[VMEM] * 3 + [HBM],
        out_specs=(VMEM,) * 3,
        scratch_shapes=[
            pltpu.SMEM(src_index.shape, jnp.int32),
            pltpu.SMEM(src_amp.shape, jnp.float32),
            pltpu.SemaphoreType.DMA((2,)),
        ],
        compiler_params=PARAMS,
        cost_estimate=cost(10 * p.e0 * wide * p.lays, 12 * wide),
    )(index, amp, src_index, in_hbm(src_amp))


def spread_kernel(p, step, row_hot, col_hot, out, total):
    total[...] = lax.dot_general(
        row_hot[step],
        col_hot[...],
        (((1,), (1,)), ((), ())),
        preferred_element_type=jnp.float32,
    )
    for lay in range(p.lays):
        lanes = slice(lay * p.cols, (lay + 1) * p.cols)
        out[lay] = (
            total[0 : p.e1, lanes]
            + total[p.e0 : p.e0 + p.e1, lanes]
            + total[2 * p.e0 : 2 * p.e0 + p.e1, lanes]
        )


def spread(p, step, row_hot, col_hot):
    wide = col_hot.shape[1]
    return pl.pallas_call(
        functools.partial(spread_kernel, p, step),
        out_shape=f32(p.lays, p.e1, p.cols),
        in_specs=[VMEM] * 2,
        out_specs=VMEM,
        scratch_shapes=[pltpu.VMEM((3 * p.e0, p.lays * p.cols), jnp.float32)],
        compiler_params=PARAMS,
        cost_estimate=cost(6 * p.e0 * wide * p.lays * p.cols, 12 * wide),
    )(row_hot, col_hot)


def advance(
    p, side, now, before, before_at, coeff, coeff_at, recv_x, recv_a, recv_b, source, added, added_at,
    out, margin, wanted=None,
):
    even = parity("grp") == 0
    g = lax.axis_index("grp")
    beyond = jnp.where(even, g > 0, g < p.n_grp - 1)
    first = lax.axis_index("gx") * p.rows - margin
    count = p.rows + 2 * margin
    lane = lax.broadcasted_iota(jnp.int32, (8, p.cols), 1)
    line = lax.broadcasted_iota(jnp.int32, (8, p.cols), 0)
    for r in range(0, count, 8):
        rows = slice(r, r + 8)
        weights = [
            [coeff[i * p.lays + lay, coeff_at + r : coeff_at + r + 8, :] for i in range(3)]
            for lay in range(p.lays)
        ]
        tall = lot_rows(p, count)
        lot = r // tall
        strip = recv_x[r - lot * tall : r - lot * tall + 8, :]
        edge = r < margin or r + 8 > p.rows + margin
        if edge:
            grid_row = first + r + line
            known = (grid_row >= 0) & (grid_row < p.nx)
        for f in range(p.fields):
            reach = margin if f == 1 else margin - MAXOFF
            if r + 8 <= margin - reach or r >= p.rows + margin + reach:
                continue
            if wanted is not None and not wanted(f, r):
                continue
            far = jnp.where(beyond, recv_b[f, rows, :], 0.0)
            near = recv_a[f, rows, :]
            below = jnp.where(even, far, near)
            above = jnp.where(even, near, far)
            mids = [
                now[f * p.lays + lay, REACH + r : REACH + r + 8, :] for lay in range(p.lays)
            ]
            stack = [below] + mids + [above]
            for lay in range(p.lays):
                plane = f * p.lays + lay
                x = mids[lay]
                mid = STENCIL[0] * x
                dxx = mid
                dyy = mid
                for j in range(1, REACH + 1):
                    dxx = dxx + STENCIL[j] * (
                        now[plane, REACH + r + j : REACH + r + j + 8, :]
                        + now[plane, REACH + r - j : REACH + r - j + 8, :]
                    )
                    at = lot * p.lot + plane * REACH
                    shift = (p.cols - j - at if side == 0 else j - at - REACH) % p.cols
                    fill = pltpu.roll(strip, shift, 1) if shift else strip
                    right = jnp.where(
                        lane < p.cols - j, pltpu.roll(x, p.cols - j, 1), fill if side == 0 else 0.0
                    )
                    left = jnp.where(lane >= j, pltpu.roll(x, j, 1), fill if side == 1 else 0.0)
                    dyy = dyy + STENCIL[j] * (right + left)
                dzz = stack[lay] + stack[lay + 2] - 2.0 * x
                w = weights[lay]
                new = (
                    2.0 * x
                    - before[plane, before_at + r : before_at + r + 8, :]
                    + (w[0] * dxx + w[1] * dyy + w[2] * dzz)
                )
                extra = added if f == 1 else source
                new = new + extra[lay, added_at + r : added_at + r + 8, :]
                if edge:
                    new = jnp.where(known, new, 0.0)
                out[plane, rows, :] = new


def cut(p, out, target, part, margin):
    start = margin + part * p.half
    for lay in range(p.lays):
        target[lay * p.half : (lay + 1) * p.half, :] = out[lay, start : start + p.half, :]
        at = p.lays * p.half + lay * p.near
        start_r = start - MAXOFF
        target[at : at + p.near, :] = out[p.lays + lay, start_r : start_r + p.near, :]


def extend(p, own, got_a, got_b):
    return pl.pallas_call(
        lambda own, got_a, got_b, out: lay_out(p, out, own, got_a, got_b),
        out_shape=f32(own.shape[0], p.e0, p.cols),
        in_specs=[VMEM] * 3,
        out_specs=VMEM,
        compiler_params=PARAMS,
        cost_estimate=cost(0, 8 * own.shape[0] * p.e0 * p.cols),
    )(own, got_a, got_b)


def first_kernel(p, now, rest, recv_x, recv_a, recv_b, source, added, out, send_x, send_a, send_b):
    gap = p.d0 - p.d1
    for side in range(2):

        @pl.when(lax.axis_index("gy") == side)
        def _():
            advance(
                p, side, now, rest, gap, rest.at[p.planes :], gap, recv_x, recv_a, recv_b,
                source.at[0], added, 0, out, p.d1,
            )

    send_edges(p, out, send_x, send_a, send_b, p.d1 - p.d2, p.e2)


def first_step(p, now, rest, edges, source, added):
    return pl.pallas_call(
        functools.partial(first_kernel, p),
        out_shape=(f32(p.planes, p.e1, p.cols), *edges_shape(p, p.e2)),
        in_specs=[VMEM] * 7,
        out_specs=(VMEM,) * 4,
        compiler_params=PARAMS,
        cost_estimate=cost(60 * p.planes * p.e1 * p.cols, 8 * p.planes * p.e1 * p.cols),
    )(now, rest, *edges, source, added)


def share_kernel(p, out, keep, give):
    for side in range(2):

        @pl.when(lax.axis_index("gy") == side)
        def _():
            cut(p, out, keep, side, p.d1)
            cut(p, out, give, 1 - side, p.d1)


def share(p, one):
    return pl.pallas_call(
        functools.partial(share_kernel, p),
        out_shape=(f32(p.gift, p.cols), f32(p.gift, p.cols)),
        in_specs=[VMEM],
        out_specs=(VMEM,) * 2,
        compiler_params=PARAMS,
        cost_estimate=cost(0, 16 * p.gift * p.cols),
    )(one)


def second_kernel(p, giving, now, before, rest, recv_x, recv_a, recv_b, source, added, *refs):
    out, share = refs[-2:]
    for side in range(2):

        def wanted(f, r, part=1 - side):
            start = p.d2 + part * p.half - (MAXOFF if f == 1 else 0)
            size = p.half + (2 * MAXOFF if f == 1 else 0)
            return (start <= r < start + size) == giving

        @pl.when(lax.axis_index("gy") == side)
        def _():
            advance(
                p, side, now, before, p.d0 - p.d2, rest.at[p.planes :], p.d0 - p.d2,
                recv_x, recv_a, recv_b, source.at[1], added, p.d1 - p.d2, out, p.d2, wanted,
            )
            cut(p, out, share, 1 - side if giving else side, p.d2)


def second_step(p, giving, now, before, rest, edges, source, added, *fields):
    return pl.pallas_call(
        functools.partial(second_kernel, p, giving),
        out_shape=(f32(p.planes, p.e2, p.cols), f32(p.gift, p.cols)),
        in_specs=[VMEM] * (8 + len(fields)),
        out_specs=(VMEM,) * 2,
        input_output_aliases={} if giving else {8: 0},
        compiler_params=PARAMS,
        cost_estimate=cost(30 * p.planes * p.e2 * p.cols, 8 * p.planes * p.e2 * p.cols),
    )(now, before, rest, *edges, source, added, *fields)


def image_kernel(p, mine, one, two, offsets, *refs):
    if mine:
        fields, out, advanced, held, order, place, sems, order_sem, done_sem = refs
    else:
        _, out, held, order, place, sems, order_sem = refs
    fetch = pltpu.make_async_copy(offsets, order, order_sem)
    fetch.start()
    b = lax.axis_index("gy")
    block = pl.multiple_of((b if mine else 1 - b) * p.cols, p.cols)
    copies = []
    if mine:
        copies.append(
            pltpu.make_async_copy(fields.at[:, pl.ds(p.d2, p.rows), :], advanced, done_sem)
        )
        copies[0].start()
    ready = 0

    def launch(d):
        copy = pltpu.make_async_copy(
            held.at[d], out.at[place[d], :, :, pl.ds(block, p.cols)], sems.at[d]
        )
        copy.start()
        copies.append(copy)

    for d in range(NOFF):
        for lay in range(p.lays):
            for r in range(0, p.half, 8):
                s = lay * p.half + r
                at = p.lays * p.half + lay * p.near + r + d
                held[d, lay, r : r + 8, :] = (
                    one[s : s + 8, :] * one[at : at + 8, :]
                    + two[s : s + 8, :] * two[at : at + 8, :]
                )
        if d < EARLY:
            continue
        if d == EARLY:
            fetch.wait()
            for k in range(NOFF):
                place[order[k] + MAXOFF] = k
        while ready <= d:
            launch(ready)
            ready += 1
    for copy in copies:
        copy.wait()


def image_call(p, mine, one, two, offsets, last):
    size = NOFF * p.lays * p.half * p.cols
    images = f32(NOFF, p.lays, p.half, p.ny)
    scratch = [
        pltpu.VMEM((NOFF, p.lays, p.half, p.cols), jnp.float32),
        pltpu.SMEM((NOFF,), jnp.int32),
        pltpu.SMEM((NOFF,), jnp.int32),
        pltpu.SemaphoreType.DMA((NOFF,)),
        pltpu.SemaphoreType.DMA,
    ]
    return pl.pallas_call(
        functools.partial(image_kernel, p, mine),
        out_shape=(images, f32(p.planes, p.rows, p.cols)) if mine else images,
        in_specs=[VMEM] * 3 + ([VMEM] if mine else [HBM]),
        out_specs=(HBM, HBM) if mine else HBM,
        scratch_shapes=scratch + ([pltpu.SemaphoreType.DMA] if mine else []),
        input_output_aliases={} if mine else {3: 0},
        compiler_params=PARAMS,
        cost_estimate=cost(3 * size, 4 * size),
    )(one, two, offsets, last)


def pairs_grp(p):
    return [(g, g ^ 1) for g in range(p.n_grp)]


def pairs_between(p):
    pairs = []
    for g in range(p.n_grp):
        to = g + 1 if g % 2 else g - 1
        for a in range(p.n_gx):
            goal = (to, a) if 0 <= to < p.n_grp else (g, a ^ 1)
            pairs.append((g * p.n_gx + a, goal[0] * p.n_gx + goal[1]))
    return pairs


def pairs_rows(p, odd):
    pairs = []
    for g in range(p.n_grp):
        for a in range(p.n_gx):
            to = a + 1 if a % 2 == odd else a - 1
            goal = (g, to) if 0 <= to < p.n_gx else (g ^ 1, a)
            pairs.append((g * p.n_gx + a, goal[0] * p.n_gx + goal[1]))
    return pairs


BESIDE = [(0, 1), (1, 0)]


def body_tile_deep(
    p, previous, current, coeff, src_index, src_amp, rec_index, rec_amp, offsets
):
    tile = (p.rows, p.cols)

    def rows_around(low, high, own):
        got_a = lax.ppermute(low, ("grp", "gx"), pairs_rows(p, 0))
        got_b = lax.ppermute(high, ("grp", "gx"), pairs_rows(p, 1))
        return own, got_a, got_b

    def edges_around(send_x, send_a, send_b):
        recv_x = lax.ppermute(send_x, "gy", BESIDE)
        recv_b = lax.ppermute(send_b, ("grp", "gx"), pairs_between(p))
        recv_a = lax.ppermute(send_a, "grp", pairs_grp(p))
        return recv_x, recv_a, recv_b

    count = rec_index.shape[0]
    wide = -(-count // 128)
    if wide * 128 > count:
        rec_index = jnp.pad(rec_index, (0, wide * 128 - count))
        rec_amp = jnp.pad(rec_amp, ((0, 0), (0, wide * 128 - count)))
    (now, rest), points = pack(
        p,
        (
            (current.reshape(p.planes, *tile),),
            (previous.reshape(p.planes, *tile), coeff.reshape(3 * p.lays, *tile)),
        ),
        (rec_index.reshape(wide, 128), rec_amp, offsets),
    )
    *points, offsets = points
    now = rows_around(*now)
    rest = rows_around(*rest)
    row_hot, col_hot, source = mark(p, *points, src_index, src_amp.T)
    added = []
    for step in range(STEPS):
        added.append(spread(p, step, row_hot, col_hot))
    whole, *edges = join(p, *now)
    edges = edges_around(*edges)
    rest = extend(p, *rest)
    one, *edges = first_step(p, whole, rest, edges, source, added[0])
    edges = edges_around(*edges)
    keep_one, give = share(p, one)
    got_one = lax.ppermute(give, "gy", BESIDE)
    inputs = (one, whole, rest, edges, source, added[1])
    two, give = second_step(p, True, *inputs)
    got_two = lax.ppermute(give, "gy", BESIDE)
    two, keep_two = second_step(p, False, *inputs, two)
    images, advanced = image_call(p, True, keep_one, keep_two, offsets, two)
    images = image_call(p, False, got_one, got_two, offsets, images)
    return images, advanced.reshape(p.fields, p.lays, *tile)


def solution(mesh):
    planned = mesh.shape["gy"] == 2 and mesh.shape["grp"] % 2 == 0 and mesh.shape["gx"] % 2 == 0

    def body(previous, *others):
        p = Plan(previous.shape, mesh.shape)
        if planned and p.fits():
            return body_tile_deep(p, previous, *others)
        return body_tiles(previous, *others)

    return jax.shard_map(
        body,
        mesh=mesh,
        in_specs=(
            P(None, "grp", "gx", "gy"),
            P(None, "grp", "gx", "gy"),
            P(None, "grp", "gx", "gy"),
            P(),
            P(),
            P(),
            P(),
            P(),
        ),
        out_specs=(P(None, "grp", ("gx", "gy"), None), P(None, "grp", "gx", "gy")),
        check_vma=False,
    )
```

```python
import functools

import jax
import jax.numpy as jnp
from jax import lax
from jax.experimental import pallas as pl
from jax.experimental.pallas import tpu as pltpu
from jax.sharding import PartitionSpec as P


STEPS = 2
NOFF = 17
MAXOFF = 8
REACH = 4


STENCIL = (-205.0 / 72.0, 8.0 / 5.0, -1.0 / 5.0, 8.0 / 315.0, -1.0 / 560.0)


def padded_2(block, sides, width):
    for axis, dim in sides:
        count = lax.axis_size(axis)
        forward = [(i, i + 1) for i in range(count - 1)]
        backward = [(target, source) for source, target in forward]
        low = lax.ppermute(
            lax.slice_in_dim(block, block.shape[dim] - width, None, axis=dim), axis, forward
        )
        high = lax.ppermute(lax.slice_in_dim(block, 0, width, axis=dim), axis, backward)
        block = jnp.concatenate([low, block, high], axis=dim)
    return block


def laplace(cur, coeff):
    wide = padded_2(cur, (("gx", 2), ("gy", 3)), 4)
    deep = padded_2(cur, (("grp", 1),), 1)
    rows = cur.shape[2]
    cols = cur.shape[3]
    dxx = STENCIL[0] * cur
    dyy = STENCIL[0] * cur
    for j in range(1, 5):
        dxx = dxx + STENCIL[j] * (
            wide[:, :, 4 + j : 4 + j + rows, 4 : 4 + cols]
            + wide[:, :, 4 - j : 4 - j + rows, 4 : 4 + cols]
        )
        dyy = dyy + STENCIL[j] * (
            wide[:, :, 4 : 4 + rows, 4 + j : 4 + j + cols]
            + wide[:, :, 4 : 4 + rows, 4 - j : 4 - j + cols]
        )
    dzz = deep[:, 2:] + deep[:, :-2] - 2.0 * cur
    return coeff[0] * dxx + coeff[1] * dyy + coeff[2] * dzz


def inject(field, index, amp):
    layers, rows, cols = field.shape
    total_rows = rows * lax.axis_size("gx")
    total_cols = cols * lax.axis_size("gy")
    layer_at = index // (total_rows * total_cols) - lax.axis_index("grp") * layers
    row_at = index // total_cols % total_rows - lax.axis_index("gx") * rows
    col_at = index % total_cols - lax.axis_index("gy") * cols
    inside = (
        (layer_at >= 0)
        & (layer_at < layers)
        & (row_at >= 0)
        & (row_at < rows)
        & (col_at >= 0)
        & (col_at < cols)
    )
    layer_at = jnp.clip(layer_at, 0, layers - 1)
    row_at = jnp.clip(row_at, 0, rows - 1)
    col_at = jnp.clip(col_at, 0, cols - 1)
    return field.at[layer_at, row_at, col_at].add(jnp.where(inside, amp, 0.0))


def correlate(source, padded, offsets, rows):
    pieces = []
    for k in range(NOFF):
        start = offsets[k] + MAXOFF
        moved = lax.dynamic_slice_in_dim(padded, start, rows, axis=2)
        pieces.append(jnp.sum(source * moved, axis=0))
    return jnp.stack(pieces)


def body_tiles(previous, current, coeff, src_index, src_amp, rec_index, rec_amp, offsets):
    prev, cur = (previous, current)
    snapshots = []
    for step in range(STEPS):
        nxt = 2.0 * cur - prev + laplace(cur, coeff)
        src_field = inject(nxt[0], src_index, src_amp[step])
        rec_field = inject(nxt[1], rec_index, rec_amp[step])
        nxt = jnp.stack([src_field, rec_field])
        snapshots.append(nxt)
        prev, cur = (cur, nxt)
    snaps = jnp.stack(snapshots)
    moved = lax.all_to_all(snaps, "gy", split_axis=3, concat_axis=4, tiled=True)
    source = moved[:, 0]
    padded = padded_2(moved[:, 1], ((("gx", "gy"), 2),), MAXOFF)
    images = correlate(source, padded, offsets, source.shape[2])
    return (images, cur)


VMEM = pl.BlockSpec(memory_space=pltpu.VMEM)
HBM = pl.BlockSpec(memory_space=pltpu.HBM)
SMEM = pl.BlockSpec(memory_space=pltpu.SMEM)
PARAMS = pltpu.CompilerParams(vmem_limit_bytes=16 << 20)


class Plan:
    def __init__(self, shape, mesh_shape):
        self.fields, self.lays, self.rows, self.cols = shape
        self.n_grp, self.n_gx, self.n_gy = (mesh_shape[k] for k in ("grp", "gx", "gy"))
        self.nx = self.rows * self.n_gx
        self.ny = self.cols * self.n_gy
        self.planes = self.fields * self.lays
        self.half = self.rows // self.n_gy
        self.d2 = MAXOFF
        self.d1 = MAXOFF + REACH
        self.d0 = MAXOFF + 2 * REACH
        self.e0 = self.rows + 2 * self.d0
        self.e1 = self.rows + 2 * self.d1
        self.e2 = self.rows + 2 * self.d2
        self.near = self.half + 2 * MAXOFF
        self.lot = self.planes * REACH
        self.lots = self.cols // self.lot
        self.gift = self.lays * (self.half + self.near)

    def fits(self):
        return (
            self.n_gy == 2
            and self.n_grp % 2 == 0
            and self.n_gx % 2 == 0
            and self.rows % 16 == 0
            and self.d0 <= self.rows
            and self.cols == 128
            and self.fields == 2
            and self.lays * self.cols <= 256
            and self.e0 <= 256
            and self.cols % self.lot == 0
            and STEPS == 2
        )


def cost(flops, moved):
    return pl.CostEstimate(flops=flops, bytes_accessed=moved, transcendentals=0)


def f32(*shape):
    return jax.ShapeDtypeStruct(shape, jnp.float32)


def in_hbm(x):
    return pltpu.with_memory_space_constraint(x, pltpu.HBM)


def parity(name):
    return lax.rem(lax.axis_index(name), 2)


def pack_kernel(p, current, previous, coeff, *refs):
    cur_low, cur_high, rest_low, rest_high, own = refs[4:9]
    sems = refs[-1]
    odd = parity("gx")
    low = pl.ds(pl.multiple_of((1 - odd) * (p.rows - p.d0), 8), p.d0)
    high = pl.ds(pl.multiple_of(odd * (p.rows - p.d0), 8), p.d0)
    first, last = pl.ds(0, p.planes), pl.ds(p.planes, coeff.shape[0])
    moves = [
        (current.at[:, low, :], cur_low),
        (current.at[:, high, :], cur_high),
        (previous.at[:, low, :], rest_low.at[first]),
        (coeff.at[:, low, :], rest_low.at[last]),
        (previous.at[:, high, :], rest_high.at[first]),
        (coeff.at[:, high, :], rest_high.at[last]),
        (current, own),
        *zip(refs[:4], refs[9:13]),
    ]
    copies = [pltpu.make_async_copy(*move, sems.at[i]) for i, move in enumerate(moves)]
    for copy in copies:
        copy.start()
    for copy in copies:
        copy.wait()


def pack(p, current, previous, coeff, smalls):
    planes = p.planes + coeff.shape[0]
    arrays = (current, previous, coeff, *smalls)
    return pl.pallas_call(
        functools.partial(pack_kernel, p),
        out_shape=(
            f32(p.planes, p.d0, p.cols),
            f32(p.planes, p.d0, p.cols),
            f32(planes, p.d0, p.cols),
            f32(planes, p.d0, p.cols),
            f32(p.planes, p.rows, p.cols),
            *(jax.ShapeDtypeStruct(x.shape, x.dtype) for x in smalls[:-1]),
            pltpu.SMEM(smalls[-1].shape, smalls[-1].dtype),
        ),
        in_specs=[HBM] * len(arrays),
        out_specs=(VMEM,) * (4 + len(smalls)) + (SMEM,),
        scratch_shapes=[pltpu.SemaphoreType.DMA((7 + len(smalls),))],
        compiler_params=PARAMS,
        cost_estimate=cost(0, 4 * p.planes * p.rows * p.cols * 3),
    )(*(in_hbm(x) for x in arrays))


def lot_rows(p, count):
    return -(-count // (8 * p.lots)) * 8


def lay_out(p, target, own, got_a, got_b):
    a = lax.axis_index("gx")
    odd = parity("gx")
    upper = pl.ds(0, p.d0)
    lower = pl.ds(p.d0 + p.rows, p.d0)
    target[:, p.d0 : p.d0 + p.rows, :] = own[...]

    @pl.when(odd == 0)
    def _():
        target[:, lower, :] = got_a[...]
        target[:, upper, :] = jnp.where(a > 0, got_b[...], 0.0)

    @pl.when(odd == 1)
    def _():
        target[:, upper, :] = got_a[...]
        target[:, lower, :] = jnp.where(a < p.n_gx - 1, got_b[...], 0.0)


def send_edges(p, whole, send_x, send_a, send_b, shift, count):
    odd = parity("grp")
    lay_a = (1 - odd) * (p.lays - 1)
    lay_b = odd * (p.lays - 1)
    for f in range(p.fields):
        send_a[f] = whole[f * p.lays + lay_a, shift : shift + count, :]
        send_b[f] = whole[f * p.lays + lay_b, shift : shift + count, :]
    b = lax.axis_index("gy")
    tall = lot_rows(p, count)
    lane = lax.broadcasted_iota(jnp.int32, (8, p.cols), 1)

    def packed(first):
        for r in range(0, tall, 8):
            block = jnp.zeros((8, p.cols), jnp.float32)
            for lot in range(p.lots):
                row = lot * tall + r
                if row >= count:
                    continue
                for plane in range(p.planes):
                    at = lot * p.lot + plane * REACH
                    moved = (at - first) % p.cols
                    x = whole[plane, shift + row : shift + row + 8, :]
                    x = pltpu.roll(x, moved, 1) if moved else x
                    block = jnp.where((lane >= at) & (lane < at + REACH), x, block)
            send_x[r : r + 8, :] = block

    @pl.when(b == 0)
    def _():
        packed(p.cols - REACH)

    @pl.when(b == 1)
    def _():
        packed(0)


def join_kernel(p, own, got_a, got_b, whole, send_x, send_a, send_b):
    lay_out(p, whole, own, got_a, got_b)
    send_edges(p, whole, send_x, send_a, send_b, p.d0 - p.d1, p.e1)


def edges_shape(p, count):
    return (f32(lot_rows(p, count), p.cols), f32(p.fields, count, p.cols), f32(p.fields, count, p.cols))


def join(p, own, got_a, got_b):
    return pl.pallas_call(
        functools.partial(join_kernel, p),
        out_shape=(f32(p.planes, p.e0, p.cols), *edges_shape(p, p.e1)),
        in_specs=[VMEM] * 3,
        out_specs=(VMEM,) * 4,
        compiler_params=PARAMS,
        cost_estimate=cost(0, 8 * p.planes * p.e0 * p.cols),
    )(own, got_a, got_b)


def whole_part(x, divisor):
    return jnp.floor((x.astype(jnp.float32) + 0.5) * (1.0 / divisor)).astype(jnp.int32)


def source_kernel(p, src_index, src_amp, source):
    first_lay = lax.axis_index("grp") * p.lays
    first_row = lax.axis_index("gx") * p.rows - p.d1
    first_col = lax.axis_index("gy") * p.cols
    source[...] = jnp.zeros((STEPS, p.lays, p.e1, p.cols), jnp.float32)
    for s in range(src_index.shape[0]):
        flat = src_index[s]
        line = lax.div(flat, p.ny)
        lay = lax.div(line, p.nx) - first_lay
        row = lax.rem(line, p.nx) - first_row
        col = lax.rem(flat, p.ny) - first_col

        @pl.when((lay >= 0) & (lay < p.lays) & (row >= 0) & (row < p.e1))
        def _():
            hit = lax.broadcasted_iota(jnp.int32, (1, p.cols), 1) == col
            for step in range(STEPS):
                source[step, lay, pl.ds(row, 1), :] += jnp.where(hit, src_amp[s, step], 0.0)


def source_map(p, src_index, src_amp):
    return pl.pallas_call(
        functools.partial(source_kernel, p),
        out_shape=f32(STEPS, p.lays, p.e1, p.cols),
        in_specs=[SMEM, SMEM],
        out_specs=VMEM,
        compiler_params=PARAMS,
        cost_estimate=cost(0, 4 * STEPS * p.lays * p.e1 * p.cols),
    )(src_index, pltpu.with_memory_space_constraint(src_amp, pltpu.SMEM))


def mark_kernel(p, index, amp, previous, coeff, row_hot, col_hot, own, sems):
    fetches = [
        pltpu.make_async_copy(previous, own.at[pl.ds(0, p.planes)], sems.at[0]),
        pltpu.make_async_copy(coeff, own.at[pl.ds(p.planes, coeff.shape[0])], sems.at[1]),
    ]
    for fetch in fetches:
        fetch.start()
    lays, stride = p.lays, p.e0
    first_lay = lax.axis_index("grp") * lays
    first_row = lax.axis_index("gx") * p.rows - p.d1
    first_col = lax.axis_index("gy") * p.cols
    narrow = jnp.bfloat16
    one, zero = jnp.ones((), narrow), jnp.zeros((), narrow)
    tall = lax.broadcasted_iota(jnp.int32, (stride, 128), 0).astype(jnp.float32).astype(narrow)
    spot = lax.broadcasted_iota(jnp.int32, (lays * p.cols, 128), 0)
    spot = spot.astype(jnp.float32).astype(narrow)

    def whole_number(x, count):
        return jnp.where((x >= 0) & (x < count), x, -1).astype(jnp.float32).astype(narrow)

    for k in range(index.shape[0]):
        at = slice(k * 128, (k + 1) * 128)
        flat = index[k : k + 1, :]
        line = whole_part(flat, p.ny)
        lay = whole_part(line, p.nx)
        row = line - lay * p.nx - first_row
        col = flat - line * p.ny - first_col
        inside = (col >= 0) & (col < p.cols)
        place = whole_number(
            jnp.where(inside, (lay - first_lay) * p.cols + col, -1), lays * p.cols
        )
        col_hot[:, at] = jnp.where(spot == place, one, zero)
        hit = tall == whole_number(row, p.e1)
        for step in range(STEPS):
            rest = amp[step : step + 1, at]
            for i in range(3):
                part = rest.astype(narrow)
                row_hot[step, i * stride : (i + 1) * stride, at] = jnp.where(hit, part, zero)
                rest = rest - part.astype(jnp.float32)
    for fetch in fetches:
        fetch.wait()


def mark(p, index, amp, previous, coeff):
    wide = index.shape[0] * 128
    return pl.pallas_call(
        functools.partial(mark_kernel, p),
        out_shape=(
            jax.ShapeDtypeStruct((STEPS, 3 * p.e0, wide), jnp.bfloat16),
            jax.ShapeDtypeStruct((p.lays * p.cols, wide), jnp.bfloat16),
            f32(p.planes + coeff.shape[0], p.rows, p.cols),
        ),
        in_specs=[VMEM] * 2 + [HBM] * 2,
        out_specs=(VMEM,) * 3,
        scratch_shapes=[pltpu.SemaphoreType.DMA((2,))],
        compiler_params=PARAMS,
        cost_estimate=cost(10 * p.e0 * wide * p.lays, 12 * wide),
    )(index, amp, in_hbm(previous), in_hbm(coeff))


def spread_kernel(p, step, row_hot, col_hot, out, total):
    total[...] = lax.dot_general(
        row_hot[step],
        col_hot[...],
        (((1,), (1,)), ((), ())),
        preferred_element_type=jnp.float32,
    )
    for lay in range(p.lays):
        lanes = slice(lay * p.cols, (lay + 1) * p.cols)
        out[lay] = (
            total[0 : p.e1, lanes]
            + total[p.e0 : p.e0 + p.e1, lanes]
            + total[2 * p.e0 : 2 * p.e0 + p.e1, lanes]
        )


def spread(p, step, row_hot, col_hot):
    wide = col_hot.shape[1]
    return pl.pallas_call(
        functools.partial(spread_kernel, p, step),
        out_shape=f32(p.lays, p.e1, p.cols),
        in_specs=[VMEM] * 2,
        out_specs=VMEM,
        scratch_shapes=[pltpu.VMEM((3 * p.e0, p.lays * p.cols), jnp.float32)],
        compiler_params=PARAMS,
        cost_estimate=cost(6 * p.e0 * wide * p.lays * p.cols, 12 * wide),
    )(row_hot, col_hot)


def advance(
    p, side, now, before, before_at, coeff, coeff_at, recv_x, recv_a, recv_b, source, added, added_at,
    out, margin, wanted=None,
):
    even = parity("grp") == 0
    g = lax.axis_index("grp")
    beyond = jnp.where(even, g > 0, g < p.n_grp - 1)
    first = lax.axis_index("gx") * p.rows - margin
    count = p.rows + 2 * margin
    lane = lax.broadcasted_iota(jnp.int32, (8, p.cols), 1)
    line = lax.broadcasted_iota(jnp.int32, (8, p.cols), 0)
    for r in range(0, count, 8):
        rows = slice(r, r + 8)
        weights = [
            [coeff[i * p.lays + lay, coeff_at + r : coeff_at + r + 8, :] for i in range(3)]
            for lay in range(p.lays)
        ]
        tall = lot_rows(p, count)
        lot = r // tall
        strip = recv_x[r - lot * tall : r - lot * tall + 8, :]
        edge = r < margin or r + 8 > p.rows + margin
        if edge:
            grid_row = first + r + line
            known = (grid_row >= 0) & (grid_row < p.nx)
        for f in range(p.fields):
            reach = margin if f == 1 else margin - MAXOFF
            if r + 8 <= margin - reach or r >= p.rows + margin + reach:
                continue
            if wanted is not None and not wanted(f, r):
                continue
            far = jnp.where(beyond, recv_b[f, rows, :], 0.0)
            near = recv_a[f, rows, :]
            below = jnp.where(even, far, near)
            above = jnp.where(even, near, far)
            mids = [
                now[f * p.lays + lay, REACH + r : REACH + r + 8, :] for lay in range(p.lays)
            ]
            stack = [below] + mids + [above]
            for lay in range(p.lays):
                plane = f * p.lays + lay
                x = mids[lay]
                mid = STENCIL[0] * x
                dxx = mid
                dyy = mid
                for j in range(1, REACH + 1):
                    dxx = dxx + STENCIL[j] * (
                        now[plane, REACH + r + j : REACH + r + j + 8, :]
                        + now[plane, REACH + r - j : REACH + r - j + 8, :]
                    )
                    at = lot * p.lot + plane * REACH
                    shift = (p.cols - j - at if side == 0 else j - at - REACH) % p.cols
                    fill = pltpu.roll(strip, shift, 1) if shift else strip
                    right = jnp.where(
                        lane < p.cols - j, pltpu.roll(x, p.cols - j, 1), fill if side == 0 else 0.0
                    )
                    left = jnp.where(lane >= j, pltpu.roll(x, j, 1), fill if side == 1 else 0.0)
                    dyy = dyy + STENCIL[j] * (right + left)
                dzz = stack[lay] + stack[lay + 2] - 2.0 * x
                w = weights[lay]
                new = (
                    2.0 * x
                    - before[plane, before_at + r : before_at + r + 8, :]
                    + (w[0] * dxx + w[1] * dyy + w[2] * dzz)
                )
                extra = added if f == 1 else source
                new = new + extra[lay, added_at + r : added_at + r + 8, :]
                if edge:
                    new = jnp.where(known, new, 0.0)
                out[plane, rows, :] = new


def cut(p, out, target, part, margin):
    start = margin + part * p.half
    for lay in range(p.lays):
        target[lay * p.half : (lay + 1) * p.half, :] = out[lay, start : start + p.half, :]
        at = p.lays * p.half + lay * p.near
        start_r = start - MAXOFF
        target[at : at + p.near, :] = out[p.lays + lay, start_r : start_r + p.near, :]


def extend(p, own, got_a, got_b):
    return pl.pallas_call(
        lambda own, got_a, got_b, out: lay_out(p, out, own, got_a, got_b),
        out_shape=f32(own.shape[0], p.e0, p.cols),
        in_specs=[VMEM] * 3,
        out_specs=VMEM,
        compiler_params=PARAMS,
        cost_estimate=cost(0, 8 * own.shape[0] * p.e0 * p.cols),
    )(own, got_a, got_b)


def first_kernel(p, now, rest, recv_x, recv_a, recv_b, source, added, out, send_x, send_a, send_b):
    gap = p.d0 - p.d1
    for side in range(2):

        @pl.when(lax.axis_index("gy") == side)
        def _():
            advance(
                p, side, now, rest, gap, rest.at[p.planes :], gap, recv_x, recv_a, recv_b,
                source.at[0], added, 0, out, p.d1,
            )

    send_edges(p, out, send_x, send_a, send_b, p.d1 - p.d2, p.e2)


def first_step(p, now, rest, edges, source, added):
    return pl.pallas_call(
        functools.partial(first_kernel, p),
        out_shape=(f32(p.planes, p.e1, p.cols), *edges_shape(p, p.e2)),
        in_specs=[VMEM] * 7,
        out_specs=(VMEM,) * 4,
        compiler_params=PARAMS,
        cost_estimate=cost(60 * p.planes * p.e1 * p.cols, 8 * p.planes * p.e1 * p.cols),
    )(now, rest, *edges, source, added)


def share_kernel(p, out, keep, give):
    for side in range(2):

        @pl.when(lax.axis_index("gy") == side)
        def _():
            cut(p, out, keep, side, p.d1)
            cut(p, out, give, 1 - side, p.d1)


def share(p, one):
    return pl.pallas_call(
        functools.partial(share_kernel, p),
        out_shape=(f32(p.gift, p.cols), f32(p.gift, p.cols)),
        in_specs=[VMEM],
        out_specs=(VMEM,) * 2,
        compiler_params=PARAMS,
        cost_estimate=cost(0, 16 * p.gift * p.cols),
    )(one)


def second_kernel(p, giving, now, before, rest, recv_x, recv_a, recv_b, source, added, *refs):
    out, share = refs[-2:]
    for side in range(2):

        def wanted(f, r, part=1 - side):
            start = p.d2 + part * p.half - (MAXOFF if f == 1 else 0)
            size = p.half + (2 * MAXOFF if f == 1 else 0)
            return (start <= r < start + size) == giving

        @pl.when(lax.axis_index("gy") == side)
        def _():
            advance(
                p, side, now, before, p.d0 - p.d2, rest.at[p.planes :], p.d0 - p.d2,
                recv_x, recv_a, recv_b, source.at[1], added, p.d1 - p.d2, out, p.d2, wanted,
            )
            cut(p, out, share, 1 - side if giving else side, p.d2)


def second_step(p, giving, now, before, rest, edges, source, added, *fields):
    return pl.pallas_call(
        functools.partial(second_kernel, p, giving),
        out_shape=(f32(p.planes, p.e2, p.cols), f32(p.gift, p.cols)),
        in_specs=[VMEM] * (8 + len(fields)),
        out_specs=(VMEM,) * 2,
        input_output_aliases={} if giving else {8: 0},
        compiler_params=PARAMS,
        cost_estimate=cost(30 * p.planes * p.e2 * p.cols, 8 * p.planes * p.e2 * p.cols),
    )(now, before, rest, *edges, source, added, *fields)


def image_kernel(p, mine, one, two, offsets, *refs):
    if mine:
        fields, out, advanced, place, held, sems, order, order_sem, done_sem = refs
        fetch = pltpu.make_async_copy(offsets, order, order_sem)
        fetch.start()
        settle = pltpu.make_async_copy(fields.at[:, pl.ds(p.d2, p.rows), :], advanced, done_sem)
        settle.start()
    else:
        place = offsets
        _, out, held, sems = refs
    b = lax.axis_index("gy")
    block = pl.multiple_of((b if mine else 1 - b) * p.cols, p.cols)
    copies = []

    def launch(d):
        copy = pltpu.make_async_copy(
            held.at[d], out.at[place[d], :, :, pl.ds(block, p.cols)], sems.at[d]
        )
        copy.start()
        copies.append(copy)

    for d in range(NOFF):
        for lay in range(p.lays):
            for r in range(0, p.half, 8):
                s = lay * p.half + r
                at = p.lays * p.half + lay * p.near + r + d
                held[d, lay, r : r + 8, :] = (
                    one[s : s + 8, :] * one[at : at + 8, :]
                    + two[s : s + 8, :] * two[at : at + 8, :]
                )
        if not mine:
            launch(d)
    if mine:
        fetch.wait()
        for k in range(NOFF):
            place[order[k] + MAXOFF] = k
        for d in range(NOFF):
            launch(d)
        settle.wait()
    for copy in copies:
        copy.wait()


def image_call(p, mine, one, two, offsets, last):
    size = NOFF * p.lays * p.half * p.cols
    images = f32(NOFF, p.lays, p.half, p.ny)
    scratch = [
        pltpu.VMEM((NOFF, p.lays, p.half, p.cols), jnp.float32),
        pltpu.SemaphoreType.DMA((NOFF,)),
    ]
    if mine:
        scratch += [
            pltpu.SMEM((NOFF,), jnp.int32),
            pltpu.SemaphoreType.DMA,
            pltpu.SemaphoreType.DMA,
        ]
        shapes = (images, f32(p.planes, p.rows, p.cols), pltpu.SMEM((NOFF,), jnp.int32))
    else:
        offsets = pltpu.with_memory_space_constraint(offsets, pltpu.SMEM)
        shapes = images
    return pl.pallas_call(
        functools.partial(image_kernel, p, mine),
        out_shape=shapes,
        in_specs=[VMEM] * 2 + ([VMEM] * 2 if mine else [SMEM, HBM]),
        out_specs=(HBM, HBM, SMEM) if mine else HBM,
        scratch_shapes=scratch,
        input_output_aliases={} if mine else {3: 0},
        compiler_params=PARAMS,
        cost_estimate=cost(3 * size, 4 * size),
    )(one, two, offsets, last)


def pairs_grp(p):
    return [(g, g ^ 1) for g in range(p.n_grp)]


def pairs_between(p):
    pairs = []
    for g in range(p.n_grp):
        to = g + 1 if g % 2 else g - 1
        for a in range(p.n_gx):
            goal = (to, a) if 0 <= to < p.n_grp else (g, a ^ 1)
            pairs.append((g * p.n_gx + a, goal[0] * p.n_gx + goal[1]))
    return pairs


def pairs_rows(p, odd):
    pairs = []
    for g in range(p.n_grp):
        for a in range(p.n_gx):
            to = a + 1 if a % 2 == odd else a - 1
            goal = (g, to) if 0 <= to < p.n_gx else (g ^ 1, a)
            pairs.append((g * p.n_gx + a, goal[0] * p.n_gx + goal[1]))
    return pairs


BESIDE = [(0, 1), (1, 0)]


def body_tile_deep(
    p, previous, current, coeff, src_index, src_amp, rec_index, rec_amp, offsets
):
    tile = (p.rows, p.cols)

    def rows_around(low, high):
        got_a = lax.ppermute(low, ("grp", "gx"), pairs_rows(p, 0))
        got_b = lax.ppermute(high, ("grp", "gx"), pairs_rows(p, 1))
        return got_a, got_b

    def edges_around(send_x, send_a, send_b):
        recv_x = lax.ppermute(send_x, "gy", BESIDE)
        recv_b = lax.ppermute(send_b, ("grp", "gx"), pairs_between(p))
        recv_a = lax.ppermute(send_a, "grp", pairs_grp(p))
        return recv_x, recv_a, recv_b

    count = rec_index.shape[0]
    wide = -(-count // 128)
    if wide * 128 > count:
        rec_index = jnp.pad(rec_index, (0, wide * 128 - count))
        rec_amp = jnp.pad(rec_amp, ((0, 0), (0, wide * 128 - count)))
    current = current.reshape(p.planes, *tile)
    previous = previous.reshape(p.planes, *tile)
    coeff = coeff.reshape(3 * p.lays, *tile)
    smalls = (rec_index.reshape(wide, 128), rec_amp, offsets, src_amp.T)
    *edges, own, rec_index, rec_amp, offsets, src_amp = pack(p, current, previous, coeff, smalls)
    now = rows_around(*edges[:2])
    rest = rows_around(*edges[2:])
    row_hot, col_hot, rest_own = mark(p, rec_index, rec_amp, previous, coeff)
    source = source_map(p, src_index, src_amp)
    added = []
    for step in range(STEPS):
        added.append(spread(p, step, row_hot, col_hot))
    whole, *edges = join(p, own, *now)
    edges = edges_around(*edges)
    rest = extend(p, rest_own, *rest)
    one, *edges = first_step(p, whole, rest, edges, source, added[0])
    edges = edges_around(*edges)
    keep_one, give = share(p, one)
    got_one = lax.ppermute(give, "gy", BESIDE)
    inputs = (one, whole, rest, edges, source, added[1])
    two, give = second_step(p, True, *inputs)
    got_two = lax.ppermute(give, "gy", BESIDE)
    two, keep_two = second_step(p, False, *inputs, two)
    images, advanced, place = image_call(p, True, keep_one, keep_two, offsets, two)
    images = image_call(p, False, got_one, got_two, place, images)
    return images, advanced.reshape(p.fields, p.lays, *tile)


def solution(mesh):
    planned = mesh.shape["gy"] == 2 and mesh.shape["grp"] % 2 == 0 and mesh.shape["gx"] % 2 == 0

    def body(previous, *others):
        p = Plan(previous.shape, mesh.shape)
        if planned and p.fits():
            return body_tile_deep(p, previous, *others)
        return body_tiles(previous, *others)

    return jax.shard_map(
        body,
        mesh=mesh,
        in_specs=(
            P(None, "grp", "gx", "gy"),
            P(None, "grp", "gx", "gy"),
            P(None, "grp", "gx", "gy"),
            P(),
            P(),
            P(),
            P(),
            P(),
        ),
        out_specs=(P(None, "grp", ("gx", "gy"), None), P(None, "grp", "gx", "gy")),
        check_vma=False,
    )
```

```python
import functools

import jax
import jax.numpy as jnp
from jax import lax
from jax.experimental import pallas as pl
from jax.experimental.pallas import tpu as pltpu
from jax.sharding import PartitionSpec as P


STEPS = 2
NOFF = 17
MAXOFF = 8
REACH = 4


STENCIL = (-205.0 / 72.0, 8.0 / 5.0, -1.0 / 5.0, 8.0 / 315.0, -1.0 / 560.0)


def padded_2(block, sides, width):
    for axis, dim in sides:
        count = lax.axis_size(axis)
        forward = [(i, i + 1) for i in range(count - 1)]
        backward = [(target, source) for source, target in forward]
        low = lax.ppermute(
            lax.slice_in_dim(block, block.shape[dim] - width, None, axis=dim), axis, forward
        )
        high = lax.ppermute(lax.slice_in_dim(block, 0, width, axis=dim), axis, backward)
        block = jnp.concatenate([low, block, high], axis=dim)
    return block


def laplace(cur, coeff):
    wide = padded_2(cur, (("gx", 2), ("gy", 3)), 4)
    deep = padded_2(cur, (("grp", 1),), 1)
    rows = cur.shape[2]
    cols = cur.shape[3]
    dxx = STENCIL[0] * cur
    dyy = STENCIL[0] * cur
    for j in range(1, 5):
        dxx = dxx + STENCIL[j] * (
            wide[:, :, 4 + j : 4 + j + rows, 4 : 4 + cols]
            + wide[:, :, 4 - j : 4 - j + rows, 4 : 4 + cols]
        )
        dyy = dyy + STENCIL[j] * (
            wide[:, :, 4 : 4 + rows, 4 + j : 4 + j + cols]
            + wide[:, :, 4 : 4 + rows, 4 - j : 4 - j + cols]
        )
    dzz = deep[:, 2:] + deep[:, :-2] - 2.0 * cur
    return coeff[0] * dxx + coeff[1] * dyy + coeff[2] * dzz


def inject(field, index, amp):
    layers, rows, cols = field.shape
    total_rows = rows * lax.axis_size("gx")
    total_cols = cols * lax.axis_size("gy")
    layer_at = index // (total_rows * total_cols) - lax.axis_index("grp") * layers
    row_at = index // total_cols % total_rows - lax.axis_index("gx") * rows
    col_at = index % total_cols - lax.axis_index("gy") * cols
    inside = (
        (layer_at >= 0)
        & (layer_at < layers)
        & (row_at >= 0)
        & (row_at < rows)
        & (col_at >= 0)
        & (col_at < cols)
    )
    layer_at = jnp.clip(layer_at, 0, layers - 1)
    row_at = jnp.clip(row_at, 0, rows - 1)
    col_at = jnp.clip(col_at, 0, cols - 1)
    return field.at[layer_at, row_at, col_at].add(jnp.where(inside, amp, 0.0))


def correlate(source, padded, offsets, rows):
    pieces = []
    for k in range(NOFF):
        start = offsets[k] + MAXOFF
        moved = lax.dynamic_slice_in_dim(padded, start, rows, axis=2)
        pieces.append(jnp.sum(source * moved, axis=0))
    return jnp.stack(pieces)


def body_tiles(previous, current, coeff, src_index, src_amp, rec_index, rec_amp, offsets):
    prev, cur = (previous, current)
    snapshots = []
    for step in range(STEPS):
        nxt = 2.0 * cur - prev + laplace(cur, coeff)
        src_field = inject(nxt[0], src_index, src_amp[step])
        rec_field = inject(nxt[1], rec_index, rec_amp[step])
        nxt = jnp.stack([src_field, rec_field])
        snapshots.append(nxt)
        prev, cur = (cur, nxt)
    snaps = jnp.stack(snapshots)
    moved = lax.all_to_all(snaps, "gy", split_axis=3, concat_axis=4, tiled=True)
    source = moved[:, 0]
    padded = padded_2(moved[:, 1], ((("gx", "gy"), 2),), MAXOFF)
    images = correlate(source, padded, offsets, source.shape[2])
    return (images, cur)


VMEM = pl.BlockSpec(memory_space=pltpu.VMEM)
HBM = pl.BlockSpec(memory_space=pltpu.HBM)
SMEM = pl.BlockSpec(memory_space=pltpu.SMEM)
PARAMS = pltpu.CompilerParams(vmem_limit_bytes=16 << 20)


class Plan:
    def __init__(self, shape, mesh_shape):
        self.fields, self.lays, self.rows, self.cols = shape
        self.n_grp, self.n_gx, self.n_gy = (mesh_shape[k] for k in ("grp", "gx", "gy"))
        self.nx = self.rows * self.n_gx
        self.ny = self.cols * self.n_gy
        self.planes = self.fields * self.lays
        self.half = self.rows // self.n_gy
        self.d2 = MAXOFF
        self.d1 = MAXOFF + REACH
        self.d0 = MAXOFF + 2 * REACH
        self.e0 = self.rows + 2 * self.d0
        self.e1 = self.rows + 2 * self.d1
        self.e2 = self.rows + 2 * self.d2
        self.near = self.half + 2 * MAXOFF
        self.lot = self.planes * REACH
        self.lots = self.cols // self.lot
        self.gift = self.lays * (self.half + self.near)

    def fits(self):
        return (
            self.n_gy == 2
            and self.n_grp % 2 == 0
            and self.n_gx % 2 == 0
            and self.rows % 16 == 0
            and self.d0 <= self.rows
            and self.cols == 128
            and self.fields == 2
            and self.lays * self.cols <= 256
            and self.e0 <= 256
            and self.cols % self.lot == 0
            and STEPS == 2
        )


def cost(flops, moved):
    return pl.CostEstimate(flops=flops, bytes_accessed=moved, transcendentals=0)


def f32(*shape):
    return jax.ShapeDtypeStruct(shape, jnp.float32)


def in_hbm(x):
    return pltpu.with_memory_space_constraint(x, pltpu.HBM)


def parity(name):
    return lax.rem(lax.axis_index(name), 2)


def pack_kernel(p, current, previous, coeff, *refs):
    cur_low, cur_high, rest_low, rest_high, own = refs[4:9]
    sems = refs[-1]
    odd = parity("gx")
    low = pl.ds(pl.multiple_of((1 - odd) * (p.rows - p.d0), 8), p.d0)
    high = pl.ds(pl.multiple_of(odd * (p.rows - p.d0), 8), p.d0)
    first, last = pl.ds(0, p.planes), pl.ds(p.planes, coeff.shape[0])
    moves = [
        (current.at[:, low, :], cur_low),
        (current.at[:, high, :], cur_high),
        (previous.at[:, low, :], rest_low.at[first]),
        (coeff.at[:, low, :], rest_low.at[last]),
        (previous.at[:, high, :], rest_high.at[first]),
        (coeff.at[:, high, :], rest_high.at[last]),
        (current, own),
        *zip(refs[:4], refs[9:13]),
    ]
    copies = [pltpu.make_async_copy(*move, sems.at[i]) for i, move in enumerate(moves)]
    for copy in copies:
        copy.start()
    for copy in copies:
        copy.wait()


def pack(p, current, previous, coeff, smalls):
    planes = p.planes + coeff.shape[0]
    arrays = (current, previous, coeff, *smalls)
    return pl.pallas_call(
        functools.partial(pack_kernel, p),
        out_shape=(
            f32(p.planes, p.d0, p.cols),
            f32(p.planes, p.d0, p.cols),
            f32(planes, p.d0, p.cols),
            f32(planes, p.d0, p.cols),
            f32(p.planes, p.rows, p.cols),
            *(jax.ShapeDtypeStruct(x.shape, x.dtype) for x in smalls[:-1]),
            pltpu.SMEM(smalls[-1].shape, smalls[-1].dtype),
        ),
        in_specs=[HBM] * len(arrays),
        out_specs=(VMEM,) * (4 + len(smalls)) + (SMEM,),
        scratch_shapes=[pltpu.SemaphoreType.DMA((7 + len(smalls),))],
        compiler_params=PARAMS,
        cost_estimate=cost(0, 4 * p.planes * p.rows * p.cols * 3),
    )(*(in_hbm(x) for x in arrays))


def lot_rows(p, count):
    return -(-count // (8 * p.lots)) * 8


def lay_out(p, target, own, got_a, got_b):
    a = lax.axis_index("gx")
    odd = parity("gx")
    upper = pl.ds(0, p.d0)
    lower = pl.ds(p.d0 + p.rows, p.d0)
    target[:, p.d0 : p.d0 + p.rows, :] = own[...]

    @pl.when(odd == 0)
    def _():
        target[:, lower, :] = got_a[...]
        target[:, upper, :] = jnp.where(a > 0, got_b[...], 0.0)

    @pl.when(odd == 1)
    def _():
        target[:, upper, :] = got_a[...]
        target[:, lower, :] = jnp.where(a < p.n_gx - 1, got_b[...], 0.0)


def send_edges(p, whole, send_x, send_a, send_b, shift, count):
    odd = parity("grp")
    lay_a = (1 - odd) * (p.lays - 1)
    lay_b = odd * (p.lays - 1)
    for f in range(p.fields):
        send_a[f] = whole[f * p.lays + lay_a, shift : shift + count, :]
        send_b[f] = whole[f * p.lays + lay_b, shift : shift + count, :]
    b = lax.axis_index("gy")
    tall = lot_rows(p, count)
    lane = lax.broadcasted_iota(jnp.int32, (8, p.cols), 1)

    def packed(first):
        for r in range(0, tall, 8):
            block = jnp.zeros((8, p.cols), jnp.float32)
            for lot in range(p.lots):
                row = lot * tall + r
                if row >= count:
                    continue
                for plane in range(p.planes):
                    at = lot * p.lot + plane * REACH
                    moved = (at - first) % p.cols
                    x = whole[plane, shift + row : shift + row + 8, :]
                    x = pltpu.roll(x, moved, 1) if moved else x
                    block = jnp.where((lane >= at) & (lane < at + REACH), x, block)
            send_x[r : r + 8, :] = block

    @pl.when(b == 0)
    def _():
        packed(p.cols - REACH)

    @pl.when(b == 1)
    def _():
        packed(0)


def join_kernel(p, own, got_a, got_b, whole, send_x, send_a, send_b):
    lay_out(p, whole, own, got_a, got_b)
    send_edges(p, whole, send_x, send_a, send_b, p.d0 - p.d1, p.e1)


def edges_shape(p, count):
    return (f32(lot_rows(p, count), p.cols), f32(p.fields, count, p.cols), f32(p.fields, count, p.cols))


def join(p, own, got_a, got_b):
    return pl.pallas_call(
        functools.partial(join_kernel, p),
        out_shape=(f32(p.planes, p.e0, p.cols), *edges_shape(p, p.e1)),
        in_specs=[VMEM] * 3,
        out_specs=(VMEM,) * 4,
        compiler_params=PARAMS,
        cost_estimate=cost(0, 8 * p.planes * p.e0 * p.cols),
    )(own, got_a, got_b)


def whole_part(x, divisor):
    return jnp.floor((x.astype(jnp.float32) + 0.5) * (1.0 / divisor)).astype(jnp.int32)


def source_kernel(p, src_index, src_amp, source):
    first_lay = lax.axis_index("grp") * p.lays
    first_row = lax.axis_index("gx") * p.rows - p.d1
    first_col = lax.axis_index("gy") * p.cols
    source[...] = jnp.zeros((STEPS, p.lays, p.e1, p.cols), jnp.float32)
    for s in range(src_index.shape[0]):
        flat = src_index[s]
        line = lax.div(flat, p.ny)
        lay = lax.div(line, p.nx) - first_lay
        row = lax.rem(line, p.nx) - first_row
        col = lax.rem(flat, p.ny) - first_col

        @pl.when((lay >= 0) & (lay < p.lays) & (row >= 0) & (row < p.e1))
        def _():
            hit = lax.broadcasted_iota(jnp.int32, (1, p.cols), 1) == col
            for step in range(STEPS):
                source[step, lay, pl.ds(row, 1), :] += jnp.where(hit, src_amp[s, step], 0.0)


def source_map(p, src_index, src_amp):
    return pl.pallas_call(
        functools.partial(source_kernel, p),
        out_shape=f32(STEPS, p.lays, p.e1, p.cols),
        in_specs=[SMEM, SMEM],
        out_specs=VMEM,
        compiler_params=PARAMS,
        cost_estimate=cost(0, 4 * STEPS * p.lays * p.e1 * p.cols),
    )(src_index, pltpu.with_memory_space_constraint(src_amp, pltpu.SMEM))


NARROW = jnp.bfloat16


def counted(size):
    count = lax.broadcasted_iota(jnp.int32, (size, 128), 0)
    return count.astype(jnp.float32).astype(NARROW)


def whole_number(x, count):
    return jnp.where((x >= 0) & (x < count), x, -1).astype(jnp.float32).astype(NARROW)


def mark_rows(p, step, index, amp, row_hot):
    first_row = lax.axis_index("gx") * p.rows - p.d1
    tall = counted(p.e0)
    zero = jnp.zeros((), NARROW)
    for k in range(index.shape[0]):
        at = slice(k * 128, (k + 1) * 128)
        line = whole_part(index[k : k + 1, :], p.ny)
        row = line - whole_part(line, p.nx) * p.nx - first_row
        hit = tall == whole_number(row, p.e1)
        rest = amp[step : step + 1, at]
        for i in range(3):
            part = rest.astype(NARROW)
            row_hot[i * p.e0 : (i + 1) * p.e0, at] = jnp.where(hit, part, zero)
            rest = rest - part.astype(jnp.float32)


def mark_columns(p, index, col_hot):
    first_lay = lax.axis_index("grp") * p.lays
    first_col = lax.axis_index("gy") * p.cols
    spot = counted(p.lays * p.cols)
    one, zero = jnp.ones((), NARROW), jnp.zeros((), NARROW)
    for k in range(index.shape[0]):
        flat = index[k : k + 1, :]
        line = whole_part(flat, p.ny)
        lay = whole_part(line, p.nx)
        col = flat - line * p.ny - first_col
        inside = (col >= 0) & (col < p.cols)
        place = whole_number(
            jnp.where(inside, (lay - first_lay) * p.cols + col, -1), p.lays * p.cols
        )
        col_hot[:, k * 128 : (k + 1) * 128] = jnp.where(spot == place, one, zero)


def gather_points(p, row_hot, col_hot, out, total):
    total[...] = lax.dot_general(
        row_hot[...],
        col_hot[...],
        (((1,), (1,)), ((), ())),
        preferred_element_type=jnp.float32,
    )
    for lay in range(p.lays):
        lanes = slice(lay * p.cols, (lay + 1) * p.cols)
        out[lay] = (
            total[0 : p.e1, lanes]
            + total[p.e0 : p.e0 + p.e1, lanes]
            + total[2 * p.e0 : 2 * p.e0 + p.e1, lanes]
        )


def spread_first_kernel(
    p, index, amp, previous, coeff, out, col_hot, own, total, row_hot, sems
):
    fetches = [
        pltpu.make_async_copy(previous, own.at[pl.ds(0, p.planes)], sems.at[0]),
        pltpu.make_async_copy(coeff, own.at[pl.ds(p.planes, coeff.shape[0])], sems.at[1]),
    ]
    for fetch in fetches:
        fetch.start()
    mark_columns(p, index, col_hot)
    mark_rows(p, 0, index, amp, row_hot)
    gather_points(p, row_hot, col_hot, out, total)
    for fetch in fetches:
        fetch.wait()


def spread_scratch(p, wide):
    return [
        pltpu.VMEM((3 * p.e0, p.lays * p.cols), jnp.float32),
        pltpu.VMEM((3 * p.e0, wide), NARROW),
    ]


def spread_first(p, index, amp, previous, coeff):
    wide = index.shape[0] * 128
    return pl.pallas_call(
        functools.partial(spread_first_kernel, p),
        out_shape=(
            f32(p.lays, p.e1, p.cols),
            jax.ShapeDtypeStruct((p.lays * p.cols, wide), NARROW),
            f32(p.planes + coeff.shape[0], p.rows, p.cols),
        ),
        in_specs=[VMEM] * 2 + [HBM] * 2,
        out_specs=(VMEM,) * 3,
        scratch_shapes=[*spread_scratch(p, wide), pltpu.SemaphoreType.DMA((2,))],
        compiler_params=PARAMS,
        cost_estimate=cost(6 * p.e0 * wide * p.lays * p.cols, 12 * wide),
    )(index, amp, in_hbm(previous), in_hbm(coeff))


def spread_later_kernel(p, step, index, amp, col_hot, out, total, row_hot):
    mark_rows(p, step, index, amp, row_hot)
    gather_points(p, row_hot, col_hot, out, total)


def spread_later(p, step, index, amp, col_hot):
    wide = index.shape[0] * 128
    return pl.pallas_call(
        functools.partial(spread_later_kernel, p, step),
        out_shape=f32(p.lays, p.e1, p.cols),
        in_specs=[VMEM] * 3,
        out_specs=VMEM,
        scratch_shapes=spread_scratch(p, wide),
        compiler_params=PARAMS,
        cost_estimate=cost(6 * p.e0 * wide * p.lays * p.cols, 12 * wide),
    )(index, amp, col_hot)


def beside_sum(p, side, strip):
    spot = lax.rem(lax.broadcasted_iota(jnp.int32, (8, p.cols), 1), REACH)
    total = STENCIL[REACH] * strip
    for i in range(1, REACH):
        moved = pltpu.roll(strip, i if side == 0 else p.cols - i, 1)
        reached = spot >= i if side == 0 else spot < REACH - i
        total = total + STENCIL[REACH - i] * jnp.where(reached, moved, 0.0)
    return total


def advance(
    p, side, now, before, before_at, coeff, coeff_at, recv_x, recv_a, recv_b, source, added, added_at,
    out, margin, wanted=None,
):
    even = parity("grp") == 0
    g = lax.axis_index("grp")
    beyond = jnp.where(even, g > 0, g < p.n_grp - 1)
    first = lax.axis_index("gx") * p.rows - margin
    count = p.rows + 2 * margin
    lane = lax.broadcasted_iota(jnp.int32, (8, p.cols), 1)
    line = lax.broadcasted_iota(jnp.int32, (8, p.cols), 0)
    tall = lot_rows(p, count)
    folded = [beside_sum(p, side, recv_x[t : t + 8, :]) for t in range(0, tall, 8)]
    border = lane >= p.cols - REACH if side == 0 else lane < REACH
    for r in range(0, count, 8):
        rows = slice(r, r + 8)
        weights = [
            [coeff[i * p.lays + lay, coeff_at + r : coeff_at + r + 8, :] for i in range(3)]
            for lay in range(p.lays)
        ]
        lot = r // tall
        strip = folded[(r - lot * tall) // 8]
        edge = r < margin or r + 8 > p.rows + margin
        if edge:
            grid_row = first + r + line
            known = (grid_row >= 0) & (grid_row < p.nx)
        for f in range(p.fields):
            reach = margin if f == 1 else margin - MAXOFF
            if r + 8 <= margin - reach or r >= p.rows + margin + reach:
                continue
            if wanted is not None and not wanted(f, r):
                continue
            far = jnp.where(beyond, recv_b[f, rows, :], 0.0)
            near = recv_a[f, rows, :]
            below = jnp.where(even, far, near)
            above = jnp.where(even, near, far)
            mids = [
                now[f * p.lays + lay, REACH + r : REACH + r + 8, :] for lay in range(p.lays)
            ]
            stack = [below] + mids + [above]
            for lay in range(p.lays):
                plane = f * p.lays + lay
                x = mids[lay]
                mid = STENCIL[0] * x
                dxx = mid
                dyy = mid
                for j in range(1, REACH + 1):
                    dxx = dxx + STENCIL[j] * (
                        now[plane, REACH + r + j : REACH + r + j + 8, :]
                        + now[plane, REACH + r - j : REACH + r - j + 8, :]
                    )
                    right = jnp.where(lane < p.cols - j, pltpu.roll(x, p.cols - j, 1), 0.0)
                    left = jnp.where(lane >= j, pltpu.roll(x, j, 1), 0.0)
                    dyy = dyy + STENCIL[j] * (right + left)
                at = lot * p.lot + plane * REACH
                shift = (p.cols - REACH - at if side == 0 else -at) % p.cols
                fill = pltpu.roll(strip, shift, 1) if shift else strip
                dyy = dyy + jnp.where(border, fill, 0.0)
                dzz = stack[lay] + stack[lay + 2] - 2.0 * x
                w = weights[lay]
                new = (
                    2.0 * x
                    - before[plane, before_at + r : before_at + r + 8, :]
                    + (w[0] * dxx + w[1] * dyy + w[2] * dzz)
                )
                extra = added if f == 1 else source
                new = new + extra[lay, added_at + r : added_at + r + 8, :]
                if edge:
                    new = jnp.where(known, new, 0.0)
                out[plane, rows, :] = new


def cut(p, out, target, part, margin):
    start = margin + part * p.half
    for lay in range(p.lays):
        target[lay * p.half : (lay + 1) * p.half, :] = out[lay, start : start + p.half, :]
        at = p.lays * p.half + lay * p.near
        start_r = start - MAXOFF
        target[at : at + p.near, :] = out[p.lays + lay, start_r : start_r + p.near, :]


def extend(p, own, got_a, got_b):
    return pl.pallas_call(
        lambda own, got_a, got_b, out: lay_out(p, out, own, got_a, got_b),
        out_shape=f32(own.shape[0], p.e0, p.cols),
        in_specs=[VMEM] * 3,
        out_specs=VMEM,
        compiler_params=PARAMS,
        cost_estimate=cost(0, 8 * own.shape[0] * p.e0 * p.cols),
    )(own, got_a, got_b)


def first_kernel(p, now, rest, recv_x, recv_a, recv_b, source, added, out, send_x, send_a, send_b):
    gap = p.d0 - p.d1
    for side in range(2):

        @pl.when(lax.axis_index("gy") == side)
        def _():
            advance(
                p, side, now, rest, gap, rest.at[p.planes :], gap, recv_x, recv_a, recv_b,
                source.at[0], added, 0, out, p.d1,
            )

    send_edges(p, out, send_x, send_a, send_b, p.d1 - p.d2, p.e2)


def first_step(p, now, rest, edges, source, added):
    return pl.pallas_call(
        functools.partial(first_kernel, p),
        out_shape=(f32(p.planes, p.e1, p.cols), *edges_shape(p, p.e2)),
        in_specs=[VMEM] * 7,
        out_specs=(VMEM,) * 4,
        compiler_params=PARAMS,
        cost_estimate=cost(60 * p.planes * p.e1 * p.cols, 8 * p.planes * p.e1 * p.cols),
    )(now, rest, *edges, source, added)


def share_kernel(p, out, keep, give):
    for side in range(2):

        @pl.when(lax.axis_index("gy") == side)
        def _():
            cut(p, out, keep, side, p.d1)
            cut(p, out, give, 1 - side, p.d1)


def share(p, one):
    return pl.pallas_call(
        functools.partial(share_kernel, p),
        out_shape=(f32(p.gift, p.cols), f32(p.gift, p.cols)),
        in_specs=[VMEM],
        out_specs=(VMEM,) * 2,
        compiler_params=PARAMS,
        cost_estimate=cost(0, 16 * p.gift * p.cols),
    )(one)


def second_kernel(p, giving, now, before, rest, recv_x, recv_a, recv_b, source, added, *refs):
    out, share = refs[-2:]
    for side in range(2):

        def wanted(f, r, part=1 - side):
            start = p.d2 + part * p.half - (MAXOFF if f == 1 else 0)
            size = p.half + (2 * MAXOFF if f == 1 else 0)
            return (start <= r < start + size) == giving

        @pl.when(lax.axis_index("gy") == side)
        def _():
            advance(
                p, side, now, before, p.d0 - p.d2, rest.at[p.planes :], p.d0 - p.d2,
                recv_x, recv_a, recv_b, source.at[1], added, p.d1 - p.d2, out, p.d2, wanted,
            )
            cut(p, out, share, 1 - side if giving else side, p.d2)


def second_step(p, giving, now, before, rest, edges, source, added, *fields):
    return pl.pallas_call(
        functools.partial(second_kernel, p, giving),
        out_shape=(f32(p.planes, p.e2, p.cols), f32(p.gift, p.cols)),
        in_specs=[VMEM] * (8 + len(fields)),
        out_specs=(VMEM,) * 2,
        input_output_aliases={} if giving else {8: 0},
        compiler_params=PARAMS,
        cost_estimate=cost(30 * p.planes * p.e2 * p.cols, 8 * p.planes * p.e2 * p.cols),
    )(now, before, rest, *edges, source, added, *fields)


def image_kernel(p, mine, one, two, offsets, *refs):
    if mine:
        fields, out, advanced, place, held, sems, order, order_sem, done_sem = refs
        fetch = pltpu.make_async_copy(offsets, order, order_sem)
        fetch.start()
        settle = pltpu.make_async_copy(fields.at[:, pl.ds(p.d2, p.rows), :], advanced, done_sem)
        settle.start()
    else:
        place = offsets
        _, out, held, sems = refs
    b = lax.axis_index("gy")
    block = pl.multiple_of((b if mine else 1 - b) * p.cols, p.cols)
    copies = []

    def launch(d):
        copy = pltpu.make_async_copy(
            held.at[d], out.at[place[d], :, :, pl.ds(block, p.cols)], sems.at[d]
        )
        copy.start()
        copies.append(copy)

    for d in range(NOFF):
        for lay in range(p.lays):
            for r in range(0, p.half, 8):
                s = lay * p.half + r
                at = p.lays * p.half + lay * p.near + r + d
                held[d, lay, r : r + 8, :] = (
                    one[s : s + 8, :] * one[at : at + 8, :]
                    + two[s : s + 8, :] * two[at : at + 8, :]
                )
        if not mine:
            launch(d)
    if mine:
        fetch.wait()
        for k in range(NOFF):
            place[order[k] + MAXOFF] = k
        for d in range(NOFF):
            launch(d)
        settle.wait()
    for copy in copies:
        copy.wait()


def image_call(p, mine, one, two, offsets, last):
    size = NOFF * p.lays * p.half * p.cols
    images = f32(NOFF, p.lays, p.half, p.ny)
    scratch = [
        pltpu.VMEM((NOFF, p.lays, p.half, p.cols), jnp.float32),
        pltpu.SemaphoreType.DMA((NOFF,)),
    ]
    if mine:
        scratch += [
            pltpu.SMEM((NOFF,), jnp.int32),
            pltpu.SemaphoreType.DMA,
            pltpu.SemaphoreType.DMA,
        ]
        shapes = (images, f32(p.planes, p.rows, p.cols), pltpu.SMEM((NOFF,), jnp.int32))
    else:
        offsets = pltpu.with_memory_space_constraint(offsets, pltpu.SMEM)
        shapes = images
    return pl.pallas_call(
        functools.partial(image_kernel, p, mine),
        out_shape=shapes,
        in_specs=[VMEM] * 2 + ([VMEM] * 2 if mine else [SMEM, HBM]),
        out_specs=(HBM, HBM, SMEM) if mine else HBM,
        scratch_shapes=scratch,
        input_output_aliases={} if mine else {3: 0},
        compiler_params=PARAMS,
        cost_estimate=cost(3 * size, 4 * size),
    )(one, two, offsets, last)


def pairs_grp(p):
    return [(g, g ^ 1) for g in range(p.n_grp)]


def pairs_between(p):
    pairs = []
    for g in range(p.n_grp):
        to = g + 1 if g % 2 else g - 1
        for a in range(p.n_gx):
            goal = (to, a) if 0 <= to < p.n_grp else (g, a ^ 1)
            pairs.append((g * p.n_gx + a, goal[0] * p.n_gx + goal[1]))
    return pairs


def pairs_rows(p, odd):
    pairs = []
    for g in range(p.n_grp):
        for a in range(p.n_gx):
            to = a + 1 if a % 2 == odd else a - 1
            goal = (g, to) if 0 <= to < p.n_gx else (g ^ 1, a)
            pairs.append((g * p.n_gx + a, goal[0] * p.n_gx + goal[1]))
    return pairs


BESIDE = [(0, 1), (1, 0)]


def body_tile_deep(
    p, previous, current, coeff, src_index, src_amp, rec_index, rec_amp, offsets
):
    tile = (p.rows, p.cols)

    def rows_around(low, high):
        got_a = lax.ppermute(low, ("grp", "gx"), pairs_rows(p, 0))
        got_b = lax.ppermute(high, ("grp", "gx"), pairs_rows(p, 1))
        return got_a, got_b

    def edges_around(send_x, send_a, send_b):
        recv_x = lax.ppermute(send_x, "gy", BESIDE)
        recv_b = lax.ppermute(send_b, ("grp", "gx"), pairs_between(p))
        recv_a = lax.ppermute(send_a, "grp", pairs_grp(p))
        return recv_x, recv_a, recv_b

    count = rec_index.shape[0]
    wide = -(-count // 128)
    if wide * 128 > count:
        rec_index = jnp.pad(rec_index, (0, wide * 128 - count))
        rec_amp = jnp.pad(rec_amp, ((0, 0), (0, wide * 128 - count)))
    current = current.reshape(p.planes, *tile)
    previous = previous.reshape(p.planes, *tile)
    coeff = coeff.reshape(3 * p.lays, *tile)
    smalls = (rec_index.reshape(wide, 128), rec_amp, offsets, src_amp.T)
    *edges, own, rec_index, rec_amp, offsets, src_amp = pack(p, current, previous, coeff, smalls)
    now = rows_around(*edges[:2])
    rest = rows_around(*edges[2:])
    source = source_map(p, src_index, src_amp)
    points = (rec_index, rec_amp)
    added_one, col_hot, rest_own = spread_first(p, *points, previous, coeff)
    added_two = spread_later(p, 1, *points, col_hot)
    whole, *edges = join(p, own, *now)
    edges = edges_around(*edges)
    rest = extend(p, rest_own, *rest)
    one, *edges = first_step(p, whole, rest, edges, source, added_one)
    edges = edges_around(*edges)
    keep_one, give = share(p, one)
    got_one = lax.ppermute(give, "gy", BESIDE)
    inputs = (one, whole, rest, edges, source, added_two)
    two, give = second_step(p, True, *inputs)
    got_two = lax.ppermute(give, "gy", BESIDE)
    two, keep_two = second_step(p, False, *inputs, two)
    images, advanced, place = image_call(p, True, keep_one, keep_two, offsets, two)
    images = image_call(p, False, got_one, got_two, place, images)
    return images, advanced.reshape(p.fields, p.lays, *tile)


def solution(mesh):
    planned = mesh.shape["gy"] == 2 and mesh.shape["grp"] % 2 == 0 and mesh.shape["gx"] % 2 == 0

    def body(previous, *others):
        p = Plan(previous.shape, mesh.shape)
        if planned and p.fits():
            return body_tile_deep(p, previous, *others)
        return body_tiles(previous, *others)

    return jax.shard_map(
        body,
        mesh=mesh,
        in_specs=(
            P(None, "grp", "gx", "gy"),
            P(None, "grp", "gx", "gy"),
            P(None, "grp", "gx", "gy"),
            P(),
            P(),
            P(),
            P(),
            P(),
        ),
        out_specs=(P(None, "grp", ("gx", "gy"), None), P(None, "grp", "gx", "gy")),
        check_vma=False,
    )
```
